32 devices in a mesh: dp: 8 (over y, x, core), mp: 4 (over z).
Axes of the slice: x: 2, y: 2, z: 4, core: 2. Of those that a mesh axis runs over, the one named last changes fastest.
Arguments:
- states: bfloat16 [512, 64, 256], P('dp', 'mp'), may hold values from -6 to 6
- key_embed: bfloat16 [512, 128], P('dp'), may hold values from -6 to 6
- partner: int32 [512], replicated, may hold values from 0 to 511, as said below
- mix_numer: int32 [512], P('dp'), may hold values from 1 to 15
- lengths: int32 [512], replicated, may hold values from 8 to 64
- w_qkv: bfloat16 [3, 256, 256], P(None, None, 'mp'), may hold values from -0.375 to 0.375
- w_out: bfloat16 [256, 256], P('mp'), may hold values from -0.375 to 0.375
- w_up: bfloat16 [256, 1024], P(None, 'mp'), may hold values from -0.375 to 0.375
- w_down: bfloat16 [1024, 256], P('mp'), may hold values from -0.1875 to 0.1875
- w_proj: bfloat16 [256, 128], replicated, may hold values from -0.375 to 0.375
Outputs:
- session_loss: float32 [512], P('dp')
- grad_states: float32 [512, 64, 256], P('dp', 'mp')
The draws below stay inside these ranges and needn't reach their ends.
Inputs may be any that keep to these rules, and one draw needn't show every extreme that they name: partner is a permutation of the 512 sessions; a session and its partner lie in different aligned blocks of 64 sessions, and at most 10 sessions of one block have their partners in one same other block.
All inputs are finite; a program needn't handle non-finite values.
Results may differ from the reference program's by a relative error of at most 0.0091.
Values may be sent and summed in bfloat16 or wider, within the bound.
A program may use at most 64 MiB of HBM per device.

```python
import jax
import jax.numpy as jnp
from jax import lax

D = 256
HEADS = 4
HD = 64
FF = 1024
E = 128
EV = 64
S_DEV = 64
INNER = 256
SESSIONS = 512
N_DP = 8


def draw_partner(key, part):
    base = jax.random.fold_in(key, 7)
    key_rank, key_slot, key_rows = jax.random.split(base, 3)
    ranks = jax.random.permutation(key_rank, S_DEV)
    shifts = 1 + ranks % (N_DP - 1)
    targets = jax.random.permutation(key_slot, S_DEV)
    row_keys = jax.random.split(key_rows, N_DP)
    orders = jax.vmap(lambda row_key: jax.random.permutation(row_key, S_DEV))(row_keys)
    devices = jnp.arange(N_DP, dtype=jnp.int32)[:, None]
    holder = (devices + shifts[orders]) % N_DP
    return (holder * S_DEV + targets[orders]).reshape(-1).astype(jnp.int32)


def touch_ends(entries, stream_key, smallest, largest):
    spot = [jax.random.randint(jax.random.fold_in(stream_key, axis), (), 0, length) for axis, length in enumerate(entries.shape)]
    widest = entries.shape.index(max(entries.shape))
    beside = spot[:widest] + [(spot[widest] + 1) % entries.shape[widest]] + spot[widest + 1:]
    return entries.at[tuple(spot)].set(smallest).at[tuple(beside)].set(largest)


def block_levels(rng, shape, cuts, least, largest):
    def one(dim, parts):
        steps = jax.random.uniform(jax.random.fold_in(jax.random.fold_in(rng, 6), dim), (parts,), jnp.float32, least / len(cuts), largest / len(cuts))
        return jnp.repeat(jnp.exp(steps), shape[dim] // parts).reshape((-1,) + (1,) * (len(shape) - dim - 1))

    gain = one(*cuts[0])
    for cut in cuts[1:]:
        gain = gain * one(*cut)
    return gain


def bell_draw(stream_key, extent, deviation, bound, cuts=(), kind=jnp.bfloat16):
    result = jax.random.normal(stream_key, extent, jnp.float32) * deviation
    if len(cuts) > 0:
        result = block_levels(stream_key, extent, cuts, -0.22, 0.18) * result
    return jnp.clip(result, min=-bound, max=bound).astype(kind)


def setup_inputs(seed: int = 0) -> dict:
    streams_of = jax.random.split(jax.random.key(seed), 11)
    states = bell_draw(streams_of[0], (SESSIONS, EV, D), 1.0, 6.0, ((0, 8), (1, 4)))
    key_embed = bell_draw(streams_of[1], (SESSIONS, E), 1.0, 6.0, ((0, 8),))
    partner = draw_partner(jax.random.fold_in(streams_of[10], 71), 0)
    mix_numer = touch_ends(jax.random.randint(streams_of[3], (SESSIONS,), 1, 16), jax.random.fold_in(streams_of[3], 1), 1, 15).astype(jnp.int32)
    lengths = touch_ends(jax.random.randint(streams_of[4], (SESSIONS,), EV // 8, EV + 1), jax.random.fold_in(streams_of[4], 1), EV // 8, EV).astype(jnp.int32)
    w_qkv = bell_draw(streams_of[5], (3, D, INNER), D ** -0.5, 0.375, ((2, 4),))
    w_out = bell_draw(streams_of[6], (INNER, D), INNER ** -0.5, 0.375, ((0, 4),))
    w_up = bell_draw(streams_of[7], (D, FF), D ** -0.5, 0.375, ((1, 4),))
    w_down = bell_draw(streams_of[8], (FF, D), FF ** -0.5, 0.1875, ((0, 4),))
    w_proj = bell_draw(streams_of[9], (D, E), D ** -0.5, 0.375)
    return dict(states=states, key_embed=key_embed, partner=partner, mix_numer=mix_numer, lengths=lengths, w_qkv=w_qkv, w_out=w_out, w_up=w_up, w_down=w_down, w_proj=w_proj)


SOFTMAX_TEMP = 0.1
LN_EPS = 1e-05
NORM_EPS = 1e-06
TOP_PRECISION = lax.Precision.HIGHEST

def rounded(values):
    return lax.optimization_barrier(values.astype(jnp.bfloat16)).astype(jnp.float32)

def layer_forward(mixed_blk, len_blk, w_qkv, w_out, w_up, w_down):
    block_size = mixed_blk.shape[0]
    row_mean = lax.optimization_barrier(jnp.mean(mixed_blk, axis=2, keepdims=True))
    centered = mixed_blk - row_mean
    inv_std = lax.rsqrt(lax.optimization_barrier(jnp.mean(centered * centered, axis=2, keepdims=True)) + LN_EPS)
    unit_rows = centered * inv_std
    normed = rounded(unit_rows)
    projected = rounded(jnp.einsum('btd,jdf->jbtf', normed, w_qkv.astype(jnp.float32)))
    projected = projected.reshape(3, block_size, EV, HEADS, HD)
    query_h = projected[0]
    key_h = projected[1]
    value_h = projected[2]
    score_scale = HD ** (-0.5)
    scores = jnp.einsum('bthc,brhc->bhtr', query_h, key_h) * score_scale
    positions = jnp.arange(EV, dtype=jnp.int32)
    token_mask = (positions[None, :] < len_blk[:, None]).astype(jnp.float32)
    exp_scores = jnp.exp(scores) * token_mask[:, None, None, :]
    probs = exp_scores / lax.optimization_barrier(jnp.sum(exp_scores, axis=3, keepdims=True))
    probs_b = rounded(probs)
    context = rounded(jnp.einsum('bhtr,brhc->bthc', probs_b, value_h)).reshape(block_size, EV, INNER)
    pre_act = jnp.einsum('btd,df->btf', normed, w_up.astype(jnp.float32))
    hidden = rounded(jax.nn.gelu(pre_act))
    branch = jnp.einsum('btf,fd->btd', context, w_out.astype(jnp.float32)) + jnp.einsum('btf,fd->btd', hidden, w_down.astype(jnp.float32))
    pool_weights = token_mask / len_blk[:, None].astype(jnp.float32)
    pooled = jnp.einsum('bt,btd->bd', pool_weights, mixed_blk + branch, precision=TOP_PRECISION)
    saved = (unit_rows, inv_std, query_h, key_h, value_h, probs, probs_b, pre_act, pool_weights)
    return (pooled, saved)

def layer_backward(mixed_blk, len_blk, grad_pooled, w_qkv, w_out, w_up, w_down):
    block_size = mixed_blk.shape[0]
    pooled, saved = layer_forward(mixed_blk, len_blk, w_qkv, w_out, w_up, w_down)
    unit_rows, inv_std, query_h, key_h, value_h, probs, probs_b, pre_act, pool_weights = saved
    grad_rows = grad_pooled[:, None, :] * pool_weights[:, :, None]
    grad_b = rounded(grad_rows)
    d_hidden = jnp.einsum('btd,fd->btf', grad_b, w_down.astype(jnp.float32))
    d_pre = rounded(jax.vjp(jax.nn.gelu, pre_act)[1](d_hidden)[0])
    d_context = rounded(jnp.einsum('btd,fd->btf', grad_b, w_out.astype(jnp.float32))).reshape(block_size, EV, HEADS, HD)
    d_value = rounded(jnp.einsum('bhtr,bthc->brhc', probs_b, d_context))
    d_prob = jnp.einsum('bthc,brhc->bhtr', d_context, value_h)
    d_score = rounded(probs * (d_prob - lax.optimization_barrier(jnp.sum(probs * d_prob, axis=3, keepdims=True))) * HD ** (-0.5))
    d_query = rounded(jnp.einsum('bhtr,brhc->bthc', d_score, key_h))
    d_key = rounded(jnp.einsum('bhtr,bthc->brhc', d_score, query_h))
    d_proj = jnp.stack([d_query, d_key, d_value]).reshape(3, block_size, EV, INNER)
    d_normed = jnp.einsum('jbtf,jdf->btd', d_proj, w_qkv.astype(jnp.float32)) + jnp.einsum('btf,df->btd', d_pre, w_up.astype(jnp.float32))
    center = lax.optimization_barrier(jnp.mean(d_normed, axis=2, keepdims=True))
    along = lax.optimization_barrier(jnp.mean(d_normed * unit_rows, axis=2, keepdims=True))
    return grad_rows + (d_normed - center - unit_rows * along) * inv_std

def reference(states, key_embed, partner, mix_numer, lengths, w_qkv, w_out, w_up, w_down, w_proj):
    mixup_weight = mix_numer.astype(jnp.float32) / 16.0
    mix_rows = mixup_weight[:, None, None]
    states_f = states.astype(jnp.float32)
    mixed = rounded(mix_rows * states_f + (1.0 - mix_rows) * states_f[partner])
    len_mix = jnp.maximum(lengths, lengths[partner])
    blocks_x = mixed.reshape(N_DP, S_DEV, EV, D)
    blocks_len = len_mix.reshape(N_DP, S_DEV)

    def forward_one(packed):
        return layer_forward(packed[0], packed[1], w_qkv, w_out, w_up, w_down)[0]
    pooled = lax.map(forward_one, (blocks_x, blocks_len)).reshape(SESSIONS, D)
    proj_f = w_proj.astype(jnp.float32)
    embed = jnp.dot(pooled, proj_f, precision=TOP_PRECISION)
    inv_norm = lax.rsqrt(lax.optimization_barrier(jnp.sum(embed * embed, axis=1, keepdims=True)) + NORM_EPS)
    unit_query_rows = embed * inv_norm
    keys_f = key_embed.astype(jnp.float32)
    unit_key_rows = keys_f * lax.rsqrt(lax.optimization_barrier(jnp.sum(keys_f * keys_f, axis=1, keepdims=True)) + NORM_EPS)
    pair_logits = jnp.dot(unit_query_rows, unit_key_rows.T, precision=TOP_PRECISION) / SOFTMAX_TEMP
    exp_logits = jnp.exp(pair_logits)
    sum_exp = lax.optimization_barrier(jnp.sum(exp_logits, axis=1))
    session_ids = jnp.arange(SESSIONS, dtype=jnp.int32)
    own_logit = jnp.take_along_axis(pair_logits, session_ids[:, None], axis=1)[:, 0]
    partner_logit = jnp.take_along_axis(pair_logits, partner[:, None], axis=1)[:, 0]
    session_loss = jnp.log(sum_exp) - mixup_weight * own_logit - (1.0 - mixup_weight) * partner_logit
    normalized_exponent = exp_logits / sum_exp[:, None]
    unit_gradient = (jnp.dot(normalized_exponent, unit_key_rows, precision=TOP_PRECISION) - mixup_weight[:, None] * unit_key_rows - (1.0 - mixup_weight)[:, None] * unit_key_rows[partner]) / SOFTMAX_TEMP
    grad_embed = (unit_gradient - unit_query_rows * lax.optimization_barrier(jnp.sum(unit_query_rows * unit_gradient, axis=1, keepdims=True))) * inv_norm
    grad_pooled = jnp.dot(grad_embed, proj_f.T, precision=TOP_PRECISION)

    def backward_one(packed):
        return layer_backward(packed[0], packed[1], packed[2], w_qkv, w_out, w_up, w_down)
    d_mixed = lax.map(backward_one, (blocks_x, blocks_len, grad_pooled.reshape(N_DP, S_DEV, D))).reshape(SESSIONS, EV, D)
    returned = rounded((1.0 - mix_rows) * d_mixed)
    inverse = jnp.argsort(partner).astype(jnp.int32)
    grad_states = mix_rows * d_mixed + returned[inverse]
    return (session_loss, grad_states)
```

```python
import functools

import jax
import jax.numpy as jnp
from jax import lax
from jax.experimental import pallas as pl
from jax.experimental.pallas import tpu as pltpu
from jax.sharding import PartitionSpec as P

HD = 64
SOFTMAX_TEMP = 0.1
LN_EPS = 1e-05
NORM_EPS = 1e-06
HIGHEST = lax.Precision.HIGHEST
MESH = pl.DeviceIdType.MESH
F32 = jnp.float32
BF16 = jnp.bfloat16


def remote(src, dst, send_sem, recv_sem, device):
    return pltpu.make_async_remote_copy(
        src_ref=src,
        dst_ref=dst,
        send_sem=send_sem,
        recv_sem=recv_sem,
        device_id=device,
        device_id_type=MESH,
    )


def greet(n, mp):
    me, mz = lax.axis_index("dp"), lax.axis_index("mp")
    barrier = pltpu.get_barrier_semaphore()
    for o in range(1, n):
        pl.semaphore_signal(
            barrier, inc=1, device_id={"dp": lax.rem(me + o, n)}, device_id_type=MESH
        )
    for o in range(1, mp):
        pl.semaphore_signal(
            barrier, inc=1, device_id={"mp": lax.rem(mz + o, mp)}, device_id_type=MESH
        )
    pl.semaphore_wait(barrier, n - 1 + mp - 1)


def gather_kernel(
    n, mp, group, cap,
    send_idx, recv_code, mix_w,
    states, keys, wts,
    mixed, all_keys, all_wts,
    out_buf, in_buf, mix_buf,
    dp_s, dp_r, key_s, key_r, mp_s, mp_r, wz_s, wz_r, wg_s, wg_r,
):
    me, mz = lax.axis_index("dp"), lax.axis_index("mp")
    sessions = states.shape[0]
    chunk = sessions // mp
    piece = wts.shape[0] // group
    part = lax.rem(me, group)
    base = me - part
    rows = pl.ds(pl.multiple_of(part * piece, piece), piece)
    greet(n, mp)

    @pl.loop(0, n * cap)
    def _(j):
        out_buf[j] = states[send_idx[j]]

    pending = []
    wz = []
    for o in range(1, mp):
        c = remote(
            wts.at[rows], all_wts.at[mz, rows], wz_s.at[o], wz_r.at[o],
            {"mp": lax.rem(mz + o, mp)},
        )
        c.start()
        wz.append(c)
    dp = []
    for o in range(1, n):
        peer = lax.rem(me + o, n)
        c = remote(
            out_buf.at[pl.ds(peer * cap, cap)], in_buf.at[pl.ds(me * cap, cap)],
            dp_s.at[o], dp_r.at[o], {"dp": peer},
        )
        c.start()
        dp.append(c)
    for o in range(1, n):
        c = remote(
            keys, all_keys.at[pl.ds(pl.multiple_of(me * sessions, sessions), sessions)],
            key_s.at[o], key_r.at[o], {"dp": lax.rem(me + o, n)},
        )
        c.start()
        pending.append(c)
    all_keys[pl.ds(pl.multiple_of(me * sessions, sessions), sessions), :] = keys[...]
    for o in range(1, mp):
        wz[o - 1].wait()
        held = lax.rem(mz + mp - o, mp)
        for g in range(1, group):
            c = remote(
                all_wts.at[held, rows], all_wts.at[held, rows],
                wg_s.at[o, g], wg_r.at[o, g], {"dp": base + lax.rem(part + g, group)},
            )
            c.start()
            pending.append(c)
    all_wts[mz] = wts[...]
    for c in dp:
        c.wait()

    @pl.loop(0, sessions)
    def _(i):
        w = mix_w[i]
        mix_buf[i] = (
            w * states[i].astype(F32) + (1.0 - w) * in_buf[recv_code[i]].astype(F32)
        ).astype(BF16)

    for o in (2, 1, 3) if mp == 4 else range(1, mp):
        peer = lax.rem(mz + o, mp)
        c = remote(
            mix_buf.at[pl.ds(peer * chunk, chunk)], mixed.at[pl.ds(0, chunk), mz],
            mp_s.at[o], mp_r.at[o], {"mp": peer},
        )
        c.start()
        pending.append(c)

    @pl.loop(0, chunk)
    def _(i):
        mixed[i, mz] = mix_buf[mz * chunk + i]

    for c in pending:
        c.wait()


def return_kernel(
    n, mp, cap,
    recv_idx, send_code, mix_w,
    dmix, loss,
    grad, all_loss,
    dm_buf, ret_buf, arr_buf,
    mp_s, mp_r, ls_s, ls_r, dp_s, dp_r,
):
    me, mz = lax.axis_index("dp"), lax.axis_index("mp")
    chunk = dmix.shape[0]
    sessions = dm_buf.shape[0]
    greet(n, mp)
    mine = pl.ds(pl.multiple_of(mz * chunk, chunk), chunk)
    first = []
    for o in (2, 1, 3) if mp == 4 else range(1, mp):
        peer = lax.rem(mz + o, mp)
        c = remote(
            dmix.at[pl.ds(0, chunk), peer], dm_buf.at[mine], mp_s.at[o], mp_r.at[o], {"mp": peer}
        )
        c.start()
        first.append(c)
        c = remote(loss, all_loss.at[mine], ls_s.at[o], ls_r.at[o], {"mp": peer})
        c.start()
        first.append(c)
    all_loss[mine, :] = loss[...]

    @pl.loop(0, chunk)
    def _(i):
        dm_buf[mz * chunk + i] = dmix[i, mz]

    for c in first:
        c.wait()

    @pl.loop(0, n * cap)
    def _(j):
        i = recv_idx[j]
        ret_buf[j] = ((1.0 - mix_w[i]) * dm_buf[i].astype(F32)).astype(BF16)

    back = []
    for o in range(1, n):
        peer = lax.rem(me + o, n)
        c = remote(
            ret_buf.at[pl.ds(peer * cap, cap)], arr_buf.at[pl.ds(me * cap, cap)],
            dp_s.at[o], dp_r.at[o], {"dp": peer},
        )
        c.start()
        back.append(c)
    for c in back:
        c.wait()

    @pl.loop(0, sessions)
    def _(s):
        grad[s] = mix_w[s] * dm_buf[s].astype(F32) + arr_buf[send_code[s]].astype(F32)


def dot(a, b, ca=1, cb=0, precision=None):
    return lax.dot_general(
        a, b, (((ca,), (cb,)), ((), ())), precision=precision, preferred_element_type=F32
    )


def dot_split(a, b, cb=0):
    hi = a.astype(BF16)
    lo = (a - hi.astype(F32)).astype(BF16)
    return dot(hi, b, 1, cb) + dot(lo, b, 1, cb)


def layer_kernel(
    events, heads, per_block,
    lens,
    mixed, wts, keys, w_proj, aux,
    dmix, loss,
    wqkv, w_out, proj, probs, slope, hpool, xpool, ctx, d_hid, d_ctx, g_row,
):
    mp = wts.shape[0]
    width = mixed.shape[1]
    sessions = lens.shape[0]
    inner = heads * HD
    part = inner // mp
    ff_part = wts.shape[1] - 4 * part - width
    up0 = 4 * part
    down0 = up0 + width
    lanes = heads * events
    block_rows = per_block * events
    for m in range(mp):
        for j in range(3):
            wqkv[j * inner + m * part : j * inner + (m + 1) * part, :] = wts[
                m, j * part : (j + 1) * part, :
            ]
        w_out[m * part : (m + 1) * part, :] = wts[m, 3 * part : 4 * part, :]
    head_mask = (
        lax.broadcasted_iota(jnp.int32, (lanes, inner), 0) // events
        == lax.broadcasted_iota(jnp.int32, (lanes, inner), 1) // HD
    )
    ones_blk = (
        lax.broadcasted_iota(jnp.int32, (lanes, lanes), 0) // events
        == lax.broadcasted_iota(jnp.int32, (lanes, lanes), 1) // events
    ).astype(F32).astype(BF16)
    row_t = lax.broadcasted_iota(jnp.int32, (events, lanes), 0)
    lane_r = lax.broadcasted_iota(jnp.int32, (events, lanes), 1) % events
    row_w = lax.broadcasted_iota(jnp.int32, (events, width), 0)
    pool_row = lax.broadcasted_iota(jnp.int32, (per_block, block_rows), 0)
    pool_lane = lax.broadcasted_iota(jnp.int32, (per_block, block_rows), 1)
    zero_b = jnp.zeros((lanes, inner), BF16)
    scale = HD ** (-0.5)
    c0 = 0.7978845608028654

    def spread(v):
        return jnp.where(head_mask, jnp.concatenate([v] * heads, axis=0), zero_b)

    def fold(full):
        kept = jnp.where(head_mask, full, 0.0)
        total = kept[0:events]
        for h in range(1, heads):
            total = total + kept[h * events : (h + 1) * events]
        return total

    def normalise(x):
        mean = jnp.mean(x, axis=1, keepdims=True)
        centered = x - mean
        inv = lax.rsqrt(jnp.mean(centered * centered, axis=1, keepdims=True) + LN_EPS)
        return centered * inv, inv

    @pl.loop(0, sessions // per_block)
    def _(b):
        rows = pl.ds(pl.multiple_of(b * block_rows, block_rows), block_rows)
        srows = pl.ds(pl.multiple_of(b * per_block, per_block), per_block)
        mixed_b = mixed[rows, :]
        unit, _inv = normalise(mixed_b.astype(F32))
        normed = unit.astype(BF16)
        qkv = dot(normed, wqkv[...], 1, 1).astype(BF16)
        proj[rows, :] = qkv
        len_col = aux[srows, 1:2]
        pool_mask = jnp.where(
            (pool_lane // events == pool_row)
            & ((pool_lane % events).astype(F32) < len_col),
            1.0,
            0.0,
        ).astype(BF16)
        xpool[srows, :] = dot(pool_mask, mixed_b) / len_col
        for m in range(mp):
            pre = dot(normed, wts[m, up0 : up0 + width, :])
            sq = pre * pre
            th = jnp.tanh(c0 * (pre + 0.044715 * (sq * pre)))
            half = 0.5 * (1.0 + th)
            act = (pre * half).astype(BF16)
            cols = slice(m * ff_part, (m + 1) * ff_part)
            slope[rows, cols] = (
                half + 0.5 * pre * (1.0 - th * th) * (c0 * (1.0 + 3 * 0.044715 * sq))
            ).astype(BF16)
            hpool[srows, cols] = dot(pool_mask, act) / len_col
        for s in range(per_block):
            length = lens[b * per_block + s]
            lo = s * events
            q = qkv[lo : lo + events, 0:inner]
            k = qkv[lo : lo + events, inner : 2 * inner]
            v = qkv[lo : lo + events, 2 * inner : 3 * inner]
            e = jnp.where(lane_r < length, jnp.exp(dot(q, spread(k), 1, 1) * scale), 0.0)
            p = e / dot_split(e, ones_blk)
            probs[pl.ds(pl.multiple_of(b * block_rows + lo, events), events), :] = p
            used = jnp.where(row_t < length, p.astype(BF16).astype(F32), 0.0)
            seen = jnp.sum(used, axis=0, keepdims=True)
            ctx[pl.ds(b * per_block + s, 1), :] = dot_split(
                jnp.broadcast_to(seen, (8, lanes)), spread(v)
            )[0:1] / length.astype(F32)

    weight, len_all = aux[:, 0:1], aux[:, 1:2]
    own_id, partner_id = aux[:, 2:3], aux[:, 3:4]
    pooled = xpool[...] + dot_split(ctx[...], w_out[...])
    for m in range(mp):
        cols = slice(m * ff_part, (m + 1) * ff_part)
        pooled = pooled + dot_split(hpool[:, cols], wts[m, down0 : down0 + ff_part, :])
    embed = dot_split(pooled, w_proj[...])
    inv_norm = lax.rsqrt(jnp.sum(embed * embed, axis=1, keepdims=True) + NORM_EPS)
    unit_q = embed * inv_norm
    keys_f = keys[...].astype(F32)
    unit_k = keys_f * lax.rsqrt(jnp.sum(keys_f * keys_f, axis=1, keepdims=True) + NORM_EPS)
    logits = dot(unit_q, unit_k, 1, 1, HIGHEST) / SOFTMAX_TEMP
    exp_l = jnp.exp(logits)
    sum_l = jnp.sum(exp_l, axis=1, keepdims=True)
    ids = lax.broadcasted_iota(jnp.int32, logits.shape, 1).astype(F32)
    wanted = jnp.where(ids == own_id, weight, 0.0) + jnp.where(
        ids == partner_id, 1.0 - weight, 0.0
    )
    loss[...] = jnp.broadcast_to(
        jnp.log(sum_l) - jnp.sum(wanted * logits, axis=1, keepdims=True), loss.shape
    )
    grad_u = dot(exp_l / sum_l - wanted, unit_k, 1, 0, HIGHEST) / SOFTMAX_TEMP
    grad_e = (grad_u - unit_q * jnp.sum(unit_q * grad_u, axis=1, keepdims=True)) * inv_norm
    g = dot_split(grad_e, w_proj[...], 1) * (1.0 / len_all)
    g_row[...] = g
    g_b = g.astype(BF16)
    for m in range(mp):
        d_hid[:, m * ff_part : (m + 1) * ff_part] = dot(
            g_b, wts[m, down0 : down0 + ff_part, :], 1, 1
        )
    d_ctx[...] = dot(g_b, w_out[...], 1, 1)

    @pl.loop(0, sessions // per_block)
    def _(b):
        rows = pl.ds(pl.multiple_of(b * block_rows, block_rows), block_rows)
        for s in range(per_block):
            i = b * per_block + s
            srow = pl.ds(i, 1)
            length = lens[i]
            here = pl.ds(pl.multiple_of(b * block_rows + s * events, events), events)
            q = proj[here, 0:inner]
            k = proj[here, inner : 2 * inner]
            v = proj[here, 2 * inner : 3 * inner]
            p = probs[here, :]
            dc = jnp.broadcast_to(d_ctx[srow, :].astype(BF16), (events, inner))
            u = dot(dc, spread(v), 1, 1)
            kept = row_t < length
            d_score = jnp.where(
                kept, p * (u - dot_split(p * u, ones_blk)) * scale, 0.0
            ).astype(BF16)
            used = jnp.where(kept, p, 0.0).astype(BF16)
            proj[here, 0:inner] = dot(d_score, spread(k)).astype(BF16)
            proj[here, inner : 2 * inner] = fold(dot(d_score, q, 0, 0)).astype(BF16)
            proj[here, 2 * inner : 3 * inner] = fold(dot(used, dc, 0, 0)).astype(BF16)
            for m in range(mp):
                cols = slice(m * ff_part, (m + 1) * ff_part)
                kept_f = lax.broadcasted_iota(jnp.int32, (events, ff_part), 0) < length
                slope[here, cols] = jnp.where(
                    kept_f, slope[here, cols].astype(F32) * d_hid[srow, cols], 0.0
                ).astype(BF16)
        dn = dot(proj[rows, :], wqkv[...])
        for m in range(mp):
            cols = slice(m * ff_part, (m + 1) * ff_part)
            dn = dn + dot(slope[rows, cols], wts[m, up0 : up0 + width, :], 1, 1)
        unit, inv = normalise(mixed[rows, :].astype(F32))
        center = jnp.mean(dn, axis=1, keepdims=True)
        along = jnp.mean(dn * unit, axis=1, keepdims=True)
        body = (dn - center - unit * along) * inv
        for s in range(per_block):
            i = b * per_block + s
            here = pl.ds(pl.multiple_of(b * block_rows + s * events, events), events)
            direct = jnp.where(row_w < lens[i], g_row[pl.ds(i, 1), :], 0.0)
            dmix[here, :] = (direct + body[s * events : (s + 1) * events]).astype(BF16)


def local(states, key_embed, partner, mix_numer, lengths, w_qkv, w_out, w_up, w_down, w_proj):
    sessions, ev_part, width = states.shape
    n = lax.axis_size("dp")
    mp = lax.axis_size("mp")
    cap = (sessions + n - 2) // (n - 1)
    slots = n * cap
    me = lax.axis_index("dp")
    mz = lax.axis_index("mp")
    total = partner.shape[0]
    chunk = sessions // mp
    events = ev_part * mp
    inner_part = w_qkv.shape[2]
    inner = inner_part * mp
    heads = inner // HD
    ff_part = w_up.shape[1]
    group = 8 if n % 8 == 0 else 1

    source = partner.reshape(n, sessions) // sessions
    ids = jnp.arange(sessions, dtype=jnp.int32)
    slot = jnp.sum(
        (
            (source[:, :, None] == source[:, None, :]) & (ids[None, None, :] < ids[None, :, None])
        ).astype(jnp.int32),
        axis=2,
    )
    code = (jnp.arange(n, dtype=jnp.int32)[:, None] * cap + slot).reshape(-1)
    rel = partner - me * sessions
    slot_ids = jnp.arange(slots, dtype=jnp.int32)
    mine = (rel >= 0) & (rel < sessions)
    send_code = jnp.sum(jnp.where(rel[None, :] == ids[:, None], code[None, :], 0), axis=1)
    send_idx = jnp.sum(
        jnp.where((code[None, :] == slot_ids[:, None]) & mine[None, :], rel[None, :], 0), axis=1
    )
    own_source = lax.dynamic_slice_in_dim(source, me, 1, 0)[0]
    recv_code = own_source * cap + lax.dynamic_slice_in_dim(slot, me, 1, 0)[0]
    recv_idx = jnp.sum(
        jnp.where(recv_code[None, :] == slot_ids[:, None], ids[None, :], 0), axis=1
    )
    weight = mix_numer.astype(F32) / 16.0
    start = me * sessions + mz * chunk
    my_partner = lax.dynamic_slice_in_dim(partner, start, chunk)
    my_len = jnp.maximum(lax.dynamic_slice_in_dim(lengths, start, chunk), lengths[my_partner])
    aux = jnp.stack(
        [
            lax.dynamic_slice_in_dim(weight, mz * chunk, chunk),
            my_len.astype(F32),
            (start + jnp.arange(chunk, dtype=jnp.int32)).astype(F32),
            my_partner.astype(F32),
        ],
        axis=1,
    )
    wts = jnp.concatenate(
        [w_qkv.transpose(0, 2, 1).reshape(3 * inner_part, width), w_out, w_up, w_down], axis=0
    )
    smem = pl.BlockSpec(memory_space=pltpu.SMEM)
    vmem = pl.BlockSpec(memory_space=pltpu.VMEM)
    dma = pltpu.SemaphoreType.DMA

    mixed, all_keys, all_wts = pl.pallas_call(
        functools.partial(gather_kernel, n, mp, group, cap),
        out_shape=(
            jax.ShapeDtypeStruct((chunk, mp, ev_part, width), BF16),
            jax.ShapeDtypeStruct((total, key_embed.shape[1]), BF16),
            jax.ShapeDtypeStruct((mp,) + wts.shape, BF16),
        ),
        in_specs=[smem] * 3 + [vmem] * 3,
        out_specs=(vmem,) * 3,
        scratch_shapes=[
            pltpu.VMEM((slots, ev_part, width), BF16),
            pltpu.VMEM((slots, ev_part, width), BF16),
            pltpu.VMEM((sessions, ev_part, width), BF16),
            dma((n,)), dma((n,)), dma((n,)), dma((n,)),
            dma((mp,)), dma((mp,)), dma((mp,)), dma((mp,)),
            dma((mp, group)), dma((mp, group)),
        ],
        compiler_params=pltpu.CompilerParams(collective_id=0, has_side_effects=True),
    )(send_idx, recv_code, weight, states, key_embed, wts)

    rows = chunk * events
    per_block = min(8, chunk)
    dmix, loss = pl.pallas_call(
        functools.partial(layer_kernel, events, heads, per_block),
        out_shape=(
            jax.ShapeDtypeStruct((rows, width), BF16),
            jax.ShapeDtypeStruct((chunk, 128), F32),
        ),
        in_specs=[smem] + [vmem] * 5,
        out_specs=(vmem, vmem),
        scratch_shapes=[
            pltpu.VMEM((3 * inner, width), BF16),
            pltpu.VMEM((inner, width), BF16),
            pltpu.VMEM((rows, 3 * inner), BF16),
            pltpu.VMEM((rows, heads * events), F32),
            pltpu.VMEM((rows, mp * ff_part), BF16),
            pltpu.VMEM((chunk, mp * ff_part), F32),
            pltpu.VMEM((chunk, width), F32),
            pltpu.VMEM((chunk, inner), F32),
            pltpu.VMEM((chunk, mp * ff_part), F32),
            pltpu.VMEM((chunk, inner), F32),
            pltpu.VMEM((chunk, width), F32),
        ],
        compiler_params=pltpu.CompilerParams(vmem_limit_bytes=56 * 1024 * 1024),
    )(my_len, mixed.reshape(rows, width), all_wts, all_keys, w_proj, aux)

    grad, all_loss = pl.pallas_call(
        functools.partial(return_kernel, n, mp, cap),
        out_shape=(
            jax.ShapeDtypeStruct((sessions, ev_part, width), F32),
            jax.ShapeDtypeStruct((sessions, 128), F32),
        ),
        in_specs=[smem] * 3 + [vmem] * 2,
        out_specs=(vmem, vmem),
        scratch_shapes=[
            pltpu.VMEM((sessions, ev_part, width), BF16),
            pltpu.VMEM((slots, ev_part, width), BF16),
            pltpu.VMEM((slots, ev_part, width), BF16),
            dma((mp,)), dma((mp,)), dma((mp,)), dma((mp,)), dma((n,)), dma((n,)),
        ],
        compiler_params=pltpu.CompilerParams(collective_id=1, has_side_effects=True),
    )(recv_idx, send_code, weight, dmix.reshape(chunk, mp, ev_part, width), loss)
    return (all_loss[:, 0], grad)


def solution(mesh):
    placed = (
        P("dp", "mp", None),
        P("dp", None),
        P(),
        P("dp"),
        P(),
        P(None, None, "mp"),
        P("mp", None),
        P(None, "mp"),
        P("mp", None),
        P(),
    )
    return jax.shard_map(
        local, mesh=mesh, in_specs=placed, out_specs=(P("dp"), P("dp", "mp", None)), check_vma=False
    )
```

```python
import functools

import jax
import jax.numpy as jnp
from jax import lax
from jax.experimental import pallas as pl
from jax.experimental.pallas import tpu as pltpu
from jax.sharding import PartitionSpec as P

HD = 64
SOFTMAX_TEMP = 0.1
LN_EPS = 1e-05
NORM_EPS = 1e-06
HIGHEST = lax.Precision.HIGHEST
MESH = pl.DeviceIdType.MESH
F32 = jnp.float32
BF16 = jnp.bfloat16


def remote(src, dst, send_sem, recv_sem, device):
    return pltpu.make_async_remote_copy(
        src_ref=src,
        dst_ref=dst,
        send_sem=send_sem,
        recv_sem=recv_sem,
        device_id=device,
        device_id_type=MESH,
    )


def greet(n, mp):
    me, mz = lax.axis_index("dp"), lax.axis_index("mp")
    barrier = pltpu.get_barrier_semaphore()
    for o in range(1, n):
        pl.semaphore_signal(
            barrier, inc=1, device_id={"dp": lax.rem(me + o, n)}, device_id_type=MESH
        )
    for o in range(1, mp):
        pl.semaphore_signal(
            barrier, inc=1, device_id={"mp": lax.rem(mz + o, mp)}, device_id_type=MESH
        )
    pl.semaphore_wait(barrier, n - 1 + mp - 1)


def gather_kernel(
    n, mp, group, cap,
    send_idx, recv_code, mix_num,
    states, keys, w_qkv, w_out, w_up, w_down,
    mixed, all_keys, all_wts,
    out_buf, in_buf, mix_buf,
    dp_s, dp_r, key_s, key_r, mp_s, mp_r, wz_s, wz_r, wg_s, wg_r,
):
    me, mz = lax.axis_index("dp"), lax.axis_index("mp")
    sessions = states.shape[0]
    chunk = sessions // mp
    piece = all_wts.shape[1] // group
    part_w = w_out.shape[0]
    width = states.shape[2]
    eye = (
        lax.broadcasted_iota(jnp.int32, (part_w, part_w), 0)
        == lax.broadcasted_iota(jnp.int32, (part_w, part_w), 1)
    ).astype(F32).astype(BF16)
    for j in range(3):
        all_wts[mz, j * part_w : (j + 1) * part_w, :] = dot(eye, w_qkv[j], 1, 1).astype(BF16)
    all_wts[mz, 3 * part_w : 4 * part_w, :] = w_out[...]
    all_wts[mz, 4 * part_w : 4 * part_w + width, :] = w_up[...]
    all_wts[mz, 4 * part_w + width :, :] = w_down[...]
    part = lax.rem(me, group)
    base = me - part
    rows = pl.ds(pl.multiple_of(part * piece, piece), piece)
    greet(n, mp)

    @pl.loop(0, n * cap)
    def _(j):
        out_buf[j] = states[send_idx[j]]

    pending = []
    wz = []
    for o in range(1, mp):
        c = remote(
            all_wts.at[mz, rows], all_wts.at[mz, rows], wz_s.at[o], wz_r.at[o],
            {"mp": lax.rem(mz + o, mp)},
        )
        c.start()
        wz.append(c)
    dp = []
    for o in range(1, n):
        peer = lax.rem(me + o, n)
        c = remote(
            out_buf.at[pl.ds(peer * cap, cap)], in_buf.at[pl.ds(me * cap, cap)],
            dp_s.at[o], dp_r.at[o], {"dp": peer},
        )
        c.start()
        dp.append(c)
    for o in range(1, n):
        c = remote(
            keys, all_keys.at[pl.ds(pl.multiple_of(me * sessions, sessions), sessions)],
            key_s.at[o], key_r.at[o], {"dp": lax.rem(me + o, n)},
        )
        c.start()
        pending.append(c)
    all_keys[pl.ds(pl.multiple_of(me * sessions, sessions), sessions), :] = keys[...]
    for c in dp:
        c.wait()

    @pl.loop(0, sessions)
    def _(i):
        w = mix_num[i].astype(F32) * 0.0625
        mix_buf[i] = (
            w * states[i].astype(F32) + (1.0 - w) * in_buf[recv_code[i]].astype(F32)
        ).astype(BF16)

    for o in (2, 1, 3) if mp == 4 else range(1, mp):
        peer = lax.rem(mz + o, mp)
        c = remote(
            mix_buf.at[pl.ds(peer * chunk, chunk)], mixed.at[pl.ds(0, chunk), mz],
            mp_s.at[o], mp_r.at[o], {"mp": peer},
        )
        c.start()
        pending.append(c)

    for o in range(1, mp):
        wz[o - 1].wait()
        held = lax.rem(mz + mp - o, mp)
        for g in range(1, group):
            c = remote(
                all_wts.at[held, rows], all_wts.at[held, rows],
                wg_s.at[o, g], wg_r.at[o, g], {"dp": base + lax.rem(part + g, group)},
            )
            c.start()
            pending.append(c)

    @pl.loop(0, chunk)
    def _(i):
        mixed[i, mz] = mix_buf[mz * chunk + i]

    for c in pending:
        c.wait()


def return_kernel(
    n, mp, cap,
    recv_idx, mix_num,
    dmix, loss,
    dm_buf, arr_buf, all_loss,
    ret_buf,
    mp_s, mp_r, ls_s, ls_r, dp_s, dp_r,
):
    me, mz = lax.axis_index("dp"), lax.axis_index("mp")
    chunk = dmix.shape[0]
    sessions = dm_buf.shape[0]
    greet(n, mp)
    mine = pl.ds(pl.multiple_of(mz * chunk, chunk), chunk)
    first = []
    for o in (2, 1, 3) if mp == 4 else range(1, mp):
        peer = lax.rem(mz + o, mp)
        c = remote(
            dmix.at[pl.ds(0, chunk), peer], dm_buf.at[mine], mp_s.at[o], mp_r.at[o], {"mp": peer}
        )
        c.start()
        first.append(c)
        c = remote(loss, all_loss.at[mine], ls_s.at[o], ls_r.at[o], {"mp": peer})
        c.start()
        first.append(c)
    all_loss[mine, :] = loss[...]

    @pl.loop(0, chunk)
    def _(i):
        dm_buf[mz * chunk + i] = dmix[i, mz]

    for c in first:
        c.wait()

    @pl.loop(0, n * cap)
    def _(j):
        i = recv_idx[j]
        ret_buf[j] = ((1.0 - mix_num[i].astype(F32) * 0.0625) * dm_buf[i].astype(F32)).astype(BF16)

    back = []
    for o in range(1, n):
        peer = lax.rem(me + o, n)
        c = remote(
            ret_buf.at[pl.ds(peer * cap, cap)], arr_buf.at[pl.ds(me * cap, cap)],
            dp_s.at[o], dp_r.at[o], {"dp": peer},
        )
        c.start()
        back.append(c)
    for c in back:
        c.wait()


def final_kernel(send_code, mix_num, dm, arr, all_loss, grad, loss):
    block = dm.shape[0]
    sessions = all_loss.shape[0]
    base = pl.program_id(0) * block
    for j in range(block):
        s = base + j
        weight = mix_num[s].astype(F32) * 0.0625
        grad[j] = weight * dm[j].astype(F32) + arr[send_code[s]].astype(F32)
    diagonal = lax.broadcasted_iota(
        jnp.int32, (sessions, sessions), 0
    ) == lax.broadcasted_iota(jnp.int32, (sessions, sessions), 1)
    loss[...] = jnp.sum(
        jnp.where(diagonal, all_loss[:, 0:sessions], 0.0), axis=0, keepdims=True
    )


def dot(a, b, ca=1, cb=0, precision=None):
    return lax.dot_general(
        a, b, (((ca,), (cb,)), ((), ())), precision=precision, preferred_element_type=F32
    )


def dot_split(a, b, cb=0):
    hi = a.astype(BF16)
    lo = (a - hi.astype(F32)).astype(BF16)
    return dot(hi, b, 1, cb) + dot(lo, b, 1, cb)


def layer_kernel(
    events, heads, per_block,
    lengths, partner, mix_num,
    mixed, wts, keys, w_proj,
    dmix, loss,
    wqkv, w_out, proj, probs, slope, hpool, xpool, ctx, d_hid, d_ctx, g_row, aux, lens,
):
    mp = wts.shape[0]
    width = mixed.shape[1]
    sessions = hpool.shape[0]
    first = lax.axis_index("mp") * sessions
    start = lax.axis_index("dp") * (mp * sessions) + first
    for i in range(sessions):
        other = partner[start + i]
        longest = jnp.maximum(lengths[start + i], lengths[other])
        lens[i] = longest
        row = slice(i, i + 1)
        shape = (1, aux.shape[2])
        aux[0, row, :] = jnp.full(shape, mix_num[first + i].astype(F32) * 0.0625, F32)
        aux[1, row, :] = jnp.full(shape, longest.astype(F32), F32)
        aux[2, row, :] = jnp.full(shape, (start + i).astype(F32), F32)
        aux[3, row, :] = jnp.full(shape, other.astype(F32), F32)
    inner = heads * HD
    part = inner // mp
    ff_part = wts.shape[1] - 4 * part - width
    up0 = 4 * part
    down0 = up0 + width
    lanes = heads * events
    block_rows = per_block * events
    for m in range(mp):
        for j in range(3):
            wqkv[j * inner + m * part : j * inner + (m + 1) * part, :] = wts[
                m, j * part : (j + 1) * part, :
            ]
        w_out[m * part : (m + 1) * part, :] = wts[m, 3 * part : 4 * part, :]
    head_mask = (
        lax.broadcasted_iota(jnp.int32, (lanes, inner), 0) // events
        == lax.broadcasted_iota(jnp.int32, (lanes, inner), 1) // HD
    )
    ones_blk = (
        lax.broadcasted_iota(jnp.int32, (lanes, lanes), 0) // events
        == lax.broadcasted_iota(jnp.int32, (lanes, lanes), 1) // events
    ).astype(F32).astype(BF16)
    row_t = lax.broadcasted_iota(jnp.int32, (events, lanes), 0)
    lane_r = lax.broadcasted_iota(jnp.int32, (events, lanes), 1) % events
    row_w = lax.broadcasted_iota(jnp.int32, (events, width), 0)
    pool_row = lax.broadcasted_iota(jnp.int32, (per_block, block_rows), 0)
    pool_lane = lax.broadcasted_iota(jnp.int32, (per_block, block_rows), 1)
    zero_b = jnp.zeros((lanes, inner), BF16)
    scale = HD ** (-0.5)
    c0 = 0.7978845608028654

    def spread(v):
        return jnp.where(head_mask, jnp.concatenate([v] * heads, axis=0), zero_b)

    def fold(full):
        kept = jnp.where(head_mask, full, 0.0)
        total = kept[0:events]
        for h in range(1, heads):
            total = total + kept[h * events : (h + 1) * events]
        return total

    def normalise(x):
        mean = jnp.mean(x, axis=1, keepdims=True)
        centered = x - mean
        inv = lax.rsqrt(jnp.mean(centered * centered, axis=1, keepdims=True) + LN_EPS)
        return centered * inv, inv

    @pl.loop(0, sessions // per_block)
    def _(b):
        rows = pl.ds(pl.multiple_of(b * block_rows, block_rows), block_rows)
        srows = pl.ds(pl.multiple_of(b * per_block, per_block), per_block)
        mixed_b = mixed[rows, :]
        unit, _inv = normalise(mixed_b.astype(F32))
        normed = unit.astype(BF16)
        qkv = dot(normed, wqkv[...], 1, 1).astype(BF16)
        proj[rows, :] = qkv
        len_col = aux[1, srows, 0:1]
        pool_mask = jnp.where(
            (pool_lane // events == pool_row)
            & ((pool_lane % events).astype(F32) < len_col),
            1.0,
            0.0,
        ).astype(BF16)
        xpool[srows, :] = dot(pool_mask, mixed_b) / len_col
        for m in range(mp):
            pre = dot(normed, wts[m, up0 : up0 + width, :])
            sq = pre * pre
            th = jnp.tanh(c0 * (pre + 0.044715 * (sq * pre)))
            half = 0.5 * (1.0 + th)
            act = (pre * half).astype(BF16)
            cols = slice(m * ff_part, (m + 1) * ff_part)
            slope[rows, cols] = (
                half + 0.5 * pre * (1.0 - th * th) * (c0 * (1.0 + 3 * 0.044715 * sq))
            ).astype(BF16)
            hpool[srows, cols] = dot(pool_mask, act) / len_col
        for s in range(per_block):
            length = lens[b * per_block + s]
            lo = s * events
            q = qkv[lo : lo + events, 0:inner]
            k = qkv[lo : lo + events, inner : 2 * inner]
            v = qkv[lo : lo + events, 2 * inner : 3 * inner]
            e = jnp.where(lane_r < length, jnp.exp(dot(q, spread(k), 1, 1) * scale), 0.0)
            p = e / dot_split(e, ones_blk)
            probs[pl.ds(pl.multiple_of(b * block_rows + lo, events), events), :] = p
            used = jnp.where(row_t < length, p.astype(BF16).astype(F32), 0.0)
            seen = jnp.sum(used, axis=0, keepdims=True)
            ctx[pl.ds(b * per_block + s, 1), :] = dot_split(
                jnp.broadcast_to(seen, (8, lanes)), spread(v)
            )[0:1] / length.astype(F32)

    weight, len_all = aux[0, :, 0:1], aux[1, :, 0:1]
    own_id, partner_id = aux[2, :, 0:1], aux[3, :, 0:1]
    pooled = xpool[...] + dot_split(ctx[...], w_out[...])
    for m in range(mp):
        cols = slice(m * ff_part, (m + 1) * ff_part)
        pooled = pooled + dot_split(hpool[:, cols], wts[m, down0 : down0 + ff_part, :])
    embed = dot_split(pooled, w_proj[...])
    inv_norm = lax.rsqrt(jnp.sum(embed * embed, axis=1, keepdims=True) + NORM_EPS)
    unit_q = embed * inv_norm
    keys_f = keys[...].astype(F32)
    unit_k = keys_f * lax.rsqrt(jnp.sum(keys_f * keys_f, axis=1, keepdims=True) + NORM_EPS)
    logits = dot(unit_q, unit_k, 1, 1, HIGHEST) / SOFTMAX_TEMP
    exp_l = jnp.exp(logits)
    sum_l = jnp.sum(exp_l, axis=1, keepdims=True)
    ids = lax.broadcasted_iota(jnp.int32, logits.shape, 1).astype(F32)
    wanted = jnp.where(ids == own_id, weight, 0.0) + jnp.where(
        ids == partner_id, 1.0 - weight, 0.0
    )
    loss[...] = jnp.broadcast_to(
        jnp.log(sum_l) - jnp.sum(wanted * logits, axis=1, keepdims=True), loss.shape
    )
    grad_u = dot(exp_l / sum_l - wanted, unit_k, 1, 0, HIGHEST) / SOFTMAX_TEMP
    grad_e = (grad_u - unit_q * jnp.sum(unit_q * grad_u, axis=1, keepdims=True)) * inv_norm
    g = dot_split(grad_e, w_proj[...], 1) * (1.0 / len_all)
    g_row[...] = g
    g_b = g.astype(BF16)
    for m in range(mp):
        d_hid[:, m * ff_part : (m + 1) * ff_part] = dot(
            g_b, wts[m, down0 : down0 + ff_part, :], 1, 1
        )
    d_ctx[...] = dot(g_b, w_out[...], 1, 1)

    @pl.loop(0, sessions // per_block)
    def _(b):
        rows = pl.ds(pl.multiple_of(b * block_rows, block_rows), block_rows)
        for s in range(per_block):
            i = b * per_block + s
            srow = pl.ds(i, 1)
            length = lens[i]
            here = pl.ds(pl.multiple_of(b * block_rows + s * events, events), events)
            q = proj[here, 0:inner]
            k = proj[here, inner : 2 * inner]
            v = proj[here, 2 * inner : 3 * inner]
            p = probs[here, :]
            dc = jnp.broadcast_to(d_ctx[srow, :].astype(BF16), (events, inner))
            u = dot(dc, spread(v), 1, 1)
            kept = row_t < length
            d_score = jnp.where(
                kept, p * (u - dot_split(p * u, ones_blk)) * scale, 0.0
            ).astype(BF16)
            used = jnp.where(kept, p, 0.0).astype(BF16)
            proj[here, 0:inner] = dot(d_score, spread(k)).astype(BF16)
            proj[here, inner : 2 * inner] = fold(dot(d_score, q, 0, 0)).astype(BF16)
            proj[here, 2 * inner : 3 * inner] = fold(dot(used, dc, 0, 0)).astype(BF16)
            for m in range(mp):
                cols = slice(m * ff_part, (m + 1) * ff_part)
                kept_f = lax.broadcasted_iota(jnp.int32, (events, ff_part), 0) < length
                slope[here, cols] = jnp.where(
                    kept_f, slope[here, cols].astype(F32) * d_hid[srow, cols], 0.0
                ).astype(BF16)
        dn = dot(proj[rows, :], wqkv[...])
        for m in range(mp):
            cols = slice(m * ff_part, (m + 1) * ff_part)
            dn = dn + dot(slope[rows, cols], wts[m, up0 : up0 + width, :], 1, 1)
        unit, inv = normalise(mixed[rows, :].astype(F32))
        center = jnp.mean(dn, axis=1, keepdims=True)
        along = jnp.mean(dn * unit, axis=1, keepdims=True)
        body = (dn - center - unit * along) * inv
        for s in range(per_block):
            i = b * per_block + s
            here = pl.ds(pl.multiple_of(b * block_rows + s * events, events), events)
            direct = jnp.where(row_w < lens[i], g_row[pl.ds(i, 1), :], 0.0)
            dmix[here, :] = (direct + body[s * events : (s + 1) * events]).astype(BF16)


def local(states, key_embed, partner, mix_numer, lengths, w_qkv, w_out, w_up, w_down, w_proj):
    sessions, ev_part, width = states.shape
    n = lax.axis_size("dp")
    mp = lax.axis_size("mp")
    cap = (sessions + n - 2) // (n - 1)
    slots = n * cap
    me = lax.axis_index("dp")
    total = partner.shape[0]
    chunk = sessions // mp
    events = ev_part * mp
    inner_part = w_qkv.shape[2]
    inner = inner_part * mp
    heads = inner // HD
    ff_part = w_up.shape[1]
    group = 8 if n % 8 == 0 else 1

    source = partner.reshape(n, sessions) // sessions
    ids = jnp.arange(sessions, dtype=jnp.int32)
    slot = jnp.sum(
        (
            (source[:, :, None] == source[:, None, :]) & (ids[None, None, :] < ids[None, :, None])
        ).astype(jnp.int32),
        axis=2,
    )
    code = (jnp.arange(n, dtype=jnp.int32)[:, None] * cap + slot).reshape(-1)
    rel = partner - me * sessions
    slot_ids = jnp.arange(slots, dtype=jnp.int32)
    mine = (rel >= 0) & (rel < sessions)
    send_code = jnp.sum(jnp.where(rel[None, :] == ids[:, None], code[None, :], 0), axis=1)
    send_idx = jnp.sum(
        jnp.where((code[None, :] == slot_ids[:, None]) & mine[None, :], rel[None, :], 0), axis=1
    )
    own_source = lax.dynamic_slice_in_dim(source, me, 1, 0)[0]
    recv_code = own_source * cap + lax.dynamic_slice_in_dim(slot, me, 1, 0)[0]
    recv_idx = jnp.sum(
        jnp.where(recv_code[None, :] == slot_ids[:, None], ids[None, :], 0), axis=1
    )
    smem = pl.BlockSpec(memory_space=pltpu.SMEM)
    vmem = pl.BlockSpec(memory_space=pltpu.VMEM)
    dma = pltpu.SemaphoreType.DMA

    mixed, all_keys, all_wts = pl.pallas_call(
        functools.partial(gather_kernel, n, mp, group, cap),
        out_shape=(
            jax.ShapeDtypeStruct((chunk, mp, ev_part, width), BF16),
            jax.ShapeDtypeStruct((total, key_embed.shape[1]), BF16),
            jax.ShapeDtypeStruct((mp, 4 * inner_part + width + ff_part, width), BF16),
        ),
        in_specs=[smem] * 3 + [vmem] * 6,
        out_specs=(vmem,) * 3,
        scratch_shapes=[
            pltpu.VMEM((slots, ev_part, width), BF16),
            pltpu.VMEM((slots, ev_part, width), BF16),
            pltpu.VMEM((sessions, ev_part, width), BF16),
            dma((n,)), dma((n,)), dma((n,)), dma((n,)),
            dma((mp,)), dma((mp,)), dma((mp,)), dma((mp,)),
            dma((mp, group)), dma((mp, group)),
        ],
        compiler_params=pltpu.CompilerParams(collective_id=0, has_side_effects=True),
    )(send_idx, recv_code, mix_numer, states, key_embed, w_qkv, w_out, w_up, w_down)

    rows = chunk * events
    per_block = min(8, chunk)
    dmix, loss = pl.pallas_call(
        functools.partial(layer_kernel, events, heads, per_block),
        out_shape=(
            jax.ShapeDtypeStruct((rows, width), BF16),
            jax.ShapeDtypeStruct((chunk, 128), F32),
        ),
        in_specs=[smem] * 3 + [vmem] * 4,
        out_specs=(vmem, vmem),
        scratch_shapes=[
            pltpu.VMEM((3 * inner, width), BF16),
            pltpu.VMEM((inner, width), BF16),
            pltpu.VMEM((rows, 3 * inner), BF16),
            pltpu.VMEM((rows, heads * events), F32),
            pltpu.VMEM((rows, mp * ff_part), BF16),
            pltpu.VMEM((chunk, mp * ff_part), F32),
            pltpu.VMEM((chunk, width), F32),
            pltpu.VMEM((chunk, inner), F32),
            pltpu.VMEM((chunk, mp * ff_part), F32),
            pltpu.VMEM((chunk, inner), F32),
            pltpu.VMEM((chunk, width), F32),
            pltpu.VMEM((4, chunk, 128), F32),
            pltpu.SMEM((chunk,), jnp.int32),
        ],
        compiler_params=pltpu.CompilerParams(vmem_limit_bytes=56 * 1024 * 1024),
    )(lengths, partner, mix_numer, mixed.reshape(rows, width), all_wts, all_keys, w_proj)

    dm_buf, arr_buf, all_loss = pl.pallas_call(
        functools.partial(return_kernel, n, mp, cap),
        out_shape=(
            jax.ShapeDtypeStruct((sessions, ev_part, width), BF16),
            jax.ShapeDtypeStruct((slots, ev_part, width), BF16),
            jax.ShapeDtypeStruct((sessions, 128), F32),
        ),
        in_specs=[smem] * 2 + [vmem] * 2,
        out_specs=(vmem,) * 3,
        scratch_shapes=[
            pltpu.VMEM((slots, ev_part, width), BF16),
            dma((mp,)), dma((mp,)), dma((mp,)), dma((mp,)), dma((n,)), dma((n,)),
        ],
        compiler_params=pltpu.CompilerParams(collective_id=1, has_side_effects=True),
    )(recv_idx, mix_numer, dmix.reshape(chunk, mp, ev_part, width), loss)

    block = chunk
    grad, loss_row = pl.pallas_call(
        final_kernel,
        grid=(sessions // block,),
        out_shape=(
            jax.ShapeDtypeStruct((sessions, ev_part, width), F32),
            jax.ShapeDtypeStruct((1, sessions), F32),
        ),
        in_specs=[
            smem,
            smem,
            pl.BlockSpec((block, ev_part, width), lambda b: (b, 0, 0)),
            pl.BlockSpec((slots, ev_part, width), lambda b: (0, 0, 0)),
            pl.BlockSpec((sessions, 128), lambda b: (0, 0)),
        ],
        out_specs=(
            pl.BlockSpec((block, ev_part, width), lambda b: (b, 0, 0)),
            pl.BlockSpec((1, sessions), lambda b: (0, 0)),
        ),
    )(send_code, mix_numer, dm_buf, arr_buf, all_loss)
    return (loss_row.reshape(sessions), grad)


def solution(mesh):
    placed = (
        P("dp", "mp", None),
        P("dp", None),
        P(),
        P("dp"),
        P(),
        P(None, None, "mp"),
        P("mp", None),
        P(None, "mp"),
        P("mp", None),
        P(),
    )
    return jax.shard_map(
        local, mesh=mesh, in_specs=placed, out_specs=(P("dp"), P("dp", "mp", None)), check_vma=False
    )
```

```python
import functools

import jax
import jax.numpy as jnp
from jax import lax
from jax.experimental import pallas as pl
from jax.experimental.pallas import tpu as pltpu
from jax.sharding import PartitionSpec as P

HD = 64
SOFTMAX_TEMP = 0.1
LN_EPS = 1e-05
NORM_EPS = 1e-06
HIGHEST = lax.Precision.HIGHEST
MESH = pl.DeviceIdType.MESH
F32 = jnp.float32
BF16 = jnp.bfloat16


def remote(src, dst, send_sem, recv_sem, device):
    return pltpu.make_async_remote_copy(
        src_ref=src,
        dst_ref=dst,
        send_sem=send_sem,
        recv_sem=recv_sem,
        device_id=device,
        device_id_type=MESH,
    )


def greet(n, mp):
    me, mz = lax.axis_index("dp"), lax.axis_index("mp")
    barrier = pltpu.get_barrier_semaphore()
    for o in range(1, n):
        pl.semaphore_signal(
            barrier, inc=1, device_id={"dp": lax.rem(me + o, n)}, device_id_type=MESH
        )
    for o in range(1, mp):
        pl.semaphore_signal(
            barrier, inc=1, device_id={"mp": lax.rem(mz + o, mp)}, device_id_type=MESH
        )
    pl.semaphore_wait(barrier, n - 1 + mp - 1)


def gather_kernel(
    n, mp, group, cap,
    send_idx, recv_code, mix_num,
    states, keys, w_qkv, w_out, w_up, w_down,
    mixed, all_keys, all_wts,
    out_buf, in_lo, in_hi, mix_buf,
    dp_s, dp_r, key_s, key_r, mp_s, mp_r, wz_s, wz_r, wg_s, wg_r, wc_s, wc_r,
):
    me, mz = lax.axis_index("dp"), lax.axis_index("mp")
    in_buf = (in_lo, in_hi)
    sessions = states.shape[0]
    half = out_buf.shape[3]
    chunk = sessions // mp
    chips = group // 2
    piece = all_wts.shape[1] // group
    part_w = w_out.shape[0]
    width = states.shape[2]
    for j in range(3):
        all_wts[mz, j * part_w : (j + 1) * part_w, :] = w_qkv[j]
    all_wts[mz, 3 * part_w : 4 * part_w, :] = w_out[...]
    all_wts[mz, 4 * part_w : 4 * part_w + width, :] = w_up[...]
    all_wts[mz, 4 * part_w + width :, :] = w_down[...]
    place = lax.rem(me, group)
    base = me - place
    core = lax.rem(place, 2)
    chip = place // 2
    core_rows = pl.ds(pl.multiple_of(core * (chips * piece), piece), chips * piece)
    rows = pl.ds(pl.multiple_of((core * chips + chip) * piece, piece), piece)

    @pl.loop(0, n * cap)
    def _(j):
        i = send_idx[j]
        for h in range(2):
            out_buf[h, j] = states[i, :, h * half : (h + 1) * half]

    greet(n, mp)
    pending = []
    wz = []
    for o in range(1, mp):
        c = remote(
            all_wts.at[mz, rows], all_wts.at[mz, rows], wz_s.at[o], wz_r.at[o],
            {"mp": lax.rem(mz + o, mp)},
        )
        c.start()
        wz.append(c)
    dp = [[], []]
    for h in range(2):
        for o in range(1, n):
            peer = lax.rem(me + o, n)
            c = remote(
                out_buf.at[h, pl.ds(peer * cap, cap)], in_buf[h].at[pl.ds(me * cap, cap)],
                dp_s.at[h, o], dp_r.at[h, o], {"dp": peer},
            )
            c.start()
            dp[h].append(c)
    key_rows = pl.ds(pl.multiple_of(me * sessions, sessions), sessions)
    for o in range(1, n):
        c = remote(
            keys, all_keys.at[key_rows], key_s.at[o], key_r.at[o], {"dp": lax.rem(me + o, n)}
        )
        c.start()
        pending.append(c)
    all_keys[key_rows, :] = keys[...]
    plane = []
    for h in range(2):
        cols = slice(h * half, (h + 1) * half)
        for c in dp[h]:
            c.wait()

        @pl.loop(0, sessions)
        def _(i):
            w = mix_num[i].astype(F32) * 0.0625
            mix_buf[h, i] = (
                w * states[i, :, cols].astype(F32)
                + (1.0 - w) * in_buf[h][recv_code[i]].astype(F32)
            ).astype(BF16)

        for o in (2, 1, 3) if mp == 4 else range(1, mp):
            peer = lax.rem(mz + o, mp)
            c = remote(
                mix_buf.at[h, pl.ds(peer * chunk, chunk)],
                mixed.at[pl.ds(0, chunk), mz, :, cols],
                mp_s.at[h, o], mp_r.at[h, o], {"mp": peer},
            )
            c.start()
            pending.append(c)
        if h == 0:
            for o in range(1, mp):
                wz[o - 1].wait()
                held = lax.rem(mz + mp - o, mp)
                for g in range(1, chips):
                    peer = base + lax.rem(chip + g, chips) * 2 + core
                    c = remote(
                        all_wts.at[held, rows], all_wts.at[held, rows],
                        wg_s.at[o, g], wg_r.at[o, g], {"dp": peer},
                    )
                    c.start()
                    plane.append(c)

        @pl.loop(0, chunk)
        def _(i):
            mixed[i, mz, :, cols] = mix_buf[h, mz * chunk + i]

    for c in plane:
        c.wait()
    for o in range(1, mp):
        held = lax.rem(mz + mp - o, mp)
        c = remote(
            all_wts.at[held, core_rows], all_wts.at[held, core_rows],
            wc_s.at[o], wc_r.at[o], {"dp": me + 1 - 2 * core},
        )
        c.start()
        pending.append(c)
    for c in pending:
        c.wait()


def return_kernel(
    n, mp, cap,
    recv_idx, mix_num,
    dmix, loss,
    dm_lo, dm_hi, arr_buf, all_loss,
    ret_buf,
    mp_s, mp_r, ls_s, ls_r, dp_s, dp_r,
):
    me, mz = lax.axis_index("dp"), lax.axis_index("mp")
    chunk = dmix.shape[0]
    dm_buf = (dm_lo, dm_hi)
    half = dm_lo.shape[2]
    greet(n, mp)
    mine = pl.ds(pl.multiple_of(mz * chunk, chunk), chunk)
    first = [[], []]
    pending = []
    for h in range(2):
        for o in (2, 1, 3) if mp == 4 else range(1, mp):
            peer = lax.rem(mz + o, mp)
            c = remote(
                dmix.at[pl.ds(0, chunk), peer, :, h * half : (h + 1) * half],
                dm_buf[h].at[mine],
                mp_s.at[h, o], mp_r.at[h, o], {"mp": peer},
            )
            c.start()
            first[h].append(c)
    for o in range(1, mp):
        c = remote(
            loss, all_loss.at[mine], ls_s.at[o], ls_r.at[o], {"mp": lax.rem(mz + o, mp)}
        )
        c.start()
        pending.append(c)
    all_loss[mine, :] = loss[...]

    @pl.loop(0, chunk)
    def _(i):
        for h in range(2):
            dm_buf[h][mz * chunk + i] = dmix[i, mz, :, h * half : (h + 1) * half]

    for h in range(2):
        for c in first[h]:
            c.wait()

        @pl.loop(0, n * cap)
        def _(j):
            i = recv_idx[j]
            ret_buf[h, j] = (
                (1.0 - mix_num[i].astype(F32) * 0.0625) * dm_buf[h][i].astype(F32)
            ).astype(BF16)

        for o in range(1, n):
            peer = lax.rem(me + o, n)
            c = remote(
                ret_buf.at[h, pl.ds(peer * cap, cap)], arr_buf.at[h, pl.ds(me * cap, cap)],
                dp_s.at[h, o], dp_r.at[h, o], {"dp": peer},
            )
            c.start()
            pending.append(c)
    for c in pending:
        c.wait()


def final_kernel(send_code, mix_num, dm_lo, dm_hi, arr, all_loss, grad, loss):
    dm = (dm_lo, dm_hi)
    block, half = dm_lo.shape[0], dm_lo.shape[2]
    sessions = all_loss.shape[0]
    base = pl.program_id(0) * block
    for j in range(block):
        s = base + j
        weight = mix_num[s].astype(F32) * 0.0625
        for h in range(2):
            grad[j, :, h * half : (h + 1) * half] = (
                weight * dm[h][j].astype(F32) + arr[h, send_code[s]].astype(F32)
            )
    diagonal = lax.broadcasted_iota(
        jnp.int32, (sessions, sessions), 0
    ) == lax.broadcasted_iota(jnp.int32, (sessions, sessions), 1)
    loss[...] = jnp.sum(
        jnp.where(diagonal, all_loss[:, 0:sessions], 0.0), axis=0, keepdims=True
    )


def dot(a, b, ca=1, cb=0, precision=None):
    return lax.dot_general(
        a, b, (((ca,), (cb,)), ((), ())), precision=precision, preferred_element_type=F32
    )


def dot_split(a, b, cb=0):
    hi = a.astype(BF16)
    lo = (a - hi.astype(F32)).astype(BF16)
    return dot(hi, b, 1, cb) + dot(lo, b, 1, cb)


def layer_kernel(
    events, heads, per_block,
    lengths, partner, mix_num,
    mixed, wts, keys, w_proj,
    dmix, loss,
    wqkv, w_out, proj, probs, slope, hpool, xpool, ctx, d_hid, d_ctx, g_row, aux, lens,
):
    mp = wts.shape[0]
    width = mixed.shape[1]
    sessions = hpool.shape[0]
    first = lax.axis_index("mp") * sessions
    start = lax.axis_index("dp") * (mp * sessions) + first
    for i in range(sessions):
        other = partner[start + i]
        longest = jnp.maximum(lengths[start + i], lengths[other])
        lens[i] = longest
        row = slice(i, i + 1)
        shape = (1, aux.shape[2])
        aux[0, row, :] = jnp.full(shape, mix_num[first + i].astype(F32) * 0.0625, F32)
        aux[1, row, :] = jnp.full(shape, longest.astype(F32), F32)
        aux[2, row, :] = jnp.full(shape, (start + i).astype(F32), F32)
        aux[3, row, :] = jnp.full(shape, other.astype(F32), F32)
    inner = heads * HD
    part = inner // mp
    ff_part = wts.shape[1] - 4 * part - width
    up0 = 4 * part
    down0 = up0 + width
    lanes = heads * events
    block_rows = per_block * events
    for m in range(mp):
        for j in range(3):
            wqkv[j * inner + m * part : j * inner + (m + 1) * part, :] = wts[
                m, j * part : (j + 1) * part, :
            ]
        w_out[m * part : (m + 1) * part, :] = wts[m, 3 * part : 4 * part, :]
    head_mask = (
        lax.broadcasted_iota(jnp.int32, (lanes, inner), 0) // events
        == lax.broadcasted_iota(jnp.int32, (lanes, inner), 1) // HD
    )
    ones_blk = (
        lax.broadcasted_iota(jnp.int32, (lanes, lanes), 0) // events
        == lax.broadcasted_iota(jnp.int32, (lanes, lanes), 1) // events
    ).astype(F32).astype(BF16)
    row_t = lax.broadcasted_iota(jnp.int32, (events, lanes), 0)
    lane_r = lax.broadcasted_iota(jnp.int32, (events, lanes), 1) % events
    row_w = lax.broadcasted_iota(jnp.int32, (events, width), 0)
    pool_row = lax.broadcasted_iota(jnp.int32, (per_block, block_rows), 0)
    pool_lane = lax.broadcasted_iota(jnp.int32, (per_block, block_rows), 1)
    zero_b = jnp.zeros((lanes, inner), BF16)
    scale = HD ** (-0.5)
    c0 = 0.7978845608028654

    def spread(v):
        return jnp.where(head_mask, jnp.concatenate([v] * heads, axis=0), zero_b)

    def fold(full):
        kept = jnp.where(head_mask, full, 0.0)
        total = kept[0:events]
        for h in range(1, heads):
            total = total + kept[h * events : (h + 1) * events]
        return total

    def normalise(x):
        mean = jnp.mean(x, axis=1, keepdims=True)
        centered = x - mean
        inv = lax.rsqrt(jnp.mean(centered * centered, axis=1, keepdims=True) + LN_EPS)
        return centered * inv, inv

    @pl.loop(0, sessions // per_block)
    def _(b):
        rows = pl.ds(pl.multiple_of(b * block_rows, block_rows), block_rows)
        srows = pl.ds(pl.multiple_of(b * per_block, per_block), per_block)
        mixed_b = mixed[rows, :]
        unit, _inv = normalise(mixed_b.astype(F32))
        normed = unit.astype(BF16)
        qkv = dot(normed, wqkv[...], 1, 1).astype(BF16)
        proj[rows, :] = qkv
        len_col = aux[1, srows, 0:1]
        pool_mask = jnp.where(
            (pool_lane // events == pool_row)
            & ((pool_lane % events).astype(F32) < len_col),
            1.0,
            0.0,
        ).astype(BF16)
        xpool[srows, :] = dot(pool_mask, mixed_b) / len_col
        for m in range(mp):
            pre = dot(normed, wts[m, up0 : up0 + width, :])
            sq = pre * pre
            th = jnp.tanh(c0 * (pre + 0.044715 * (sq * pre)))
            half = 0.5 * (1.0 + th)
            act = (pre * half).astype(BF16)
            cols = slice(m * ff_part, (m + 1) * ff_part)
            slope[rows, cols] = (
                half + 0.5 * pre * (1.0 - th * th) * (c0 * (1.0 + 3 * 0.044715 * sq))
            ).astype(BF16)
            hpool[srows, cols] = dot(pool_mask, act) / len_col
        for s in range(per_block):
            length = lens[b * per_block + s]
            lo = s * events
            q = qkv[lo : lo + events, 0:inner]
            k = qkv[lo : lo + events, inner : 2 * inner]
            v = qkv[lo : lo + events, 2 * inner : 3 * inner]
            e = jnp.where(lane_r < length, jnp.exp(dot(q, spread(k), 1, 1) * scale), 0.0)
            p = e / dot_split(e, ones_blk)
            probs[pl.ds(pl.multiple_of(b * block_rows + lo, events), events), :] = p
            used = jnp.where(row_t < length, p.astype(BF16).astype(F32), 0.0)
            seen = jnp.sum(used, axis=0, keepdims=True)
            ctx[pl.ds(b * per_block + s, 1), :] = dot_split(
                jnp.broadcast_to(seen, (8, lanes)), spread(v)
            )[0:1] / length.astype(F32)

    weight, len_all = aux[0, :, 0:1], aux[1, :, 0:1]
    own_id, partner_id = aux[2, :, 0:1], aux[3, :, 0:1]
    pooled = xpool[...] + dot_split(ctx[...], w_out[...])
    for m in range(mp):
        cols = slice(m * ff_part, (m + 1) * ff_part)
        pooled = pooled + dot_split(hpool[:, cols], wts[m, down0 : down0 + ff_part, :])
    embed = dot_split(pooled, w_proj[...])
    inv_norm = lax.rsqrt(jnp.sum(embed * embed, axis=1, keepdims=True) + NORM_EPS)
    unit_q = embed * inv_norm
    keys_f = keys[...].astype(F32)
    unit_k = keys_f * lax.rsqrt(jnp.sum(keys_f * keys_f, axis=1, keepdims=True) + NORM_EPS)
    logits = dot(unit_q, unit_k, 1, 1, HIGHEST) / SOFTMAX_TEMP
    exp_l = jnp.exp(logits)
    sum_l = jnp.sum(exp_l, axis=1, keepdims=True)
    ids = lax.broadcasted_iota(jnp.int32, logits.shape, 1).astype(F32)
    wanted = jnp.where(ids == own_id, weight, 0.0) + jnp.where(
        ids == partner_id, 1.0 - weight, 0.0
    )
    loss[...] = jnp.broadcast_to(
        jnp.log(sum_l) - jnp.sum(wanted * logits, axis=1, keepdims=True), loss.shape
    )
    grad_u = dot(exp_l / sum_l - wanted, unit_k, 1, 0, HIGHEST) / SOFTMAX_TEMP
    grad_e = (grad_u - unit_q * jnp.sum(unit_q * grad_u, axis=1, keepdims=True)) * inv_norm
    g = dot_split(grad_e, w_proj[...], 1) * (1.0 / len_all)
    g_row[...] = g
    g_b = g.astype(BF16)
    for m in range(mp):
        d_hid[:, m * ff_part : (m + 1) * ff_part] = dot(
            g_b, wts[m, down0 : down0 + ff_part, :], 1, 1
        )
    d_ctx[...] = dot(g_b, w_out[...], 1, 1)

    @pl.loop(0, sessions // per_block)
    def _(b):
        rows = pl.ds(pl.multiple_of(b * block_rows, block_rows), block_rows)
        for s in range(per_block):
            i = b * per_block + s
            srow = pl.ds(i, 1)
            length = lens[i]
            here = pl.ds(pl.multiple_of(b * block_rows + s * events, events), events)
            q = proj[here, 0:inner]
            k = proj[here, inner : 2 * inner]
            v = proj[here, 2 * inner : 3 * inner]
            p = probs[here, :]
            dc = jnp.broadcast_to(d_ctx[srow, :].astype(BF16), (events, inner))
            u = dot(dc, spread(v), 1, 1)
            kept = row_t < length
            d_score = jnp.where(
                kept, p * (u - dot_split(p * u, ones_blk)) * scale, 0.0
            ).astype(BF16)
            used = jnp.where(kept, p, 0.0).astype(BF16)
            proj[here, 0:inner] = dot(d_score, spread(k)).astype(BF16)
            proj[here, inner : 2 * inner] = fold(dot(d_score, q, 0, 0)).astype(BF16)
            proj[here, 2 * inner : 3 * inner] = fold(dot(used, dc, 0, 0)).astype(BF16)
            for m in range(mp):
                cols = slice(m * ff_part, (m + 1) * ff_part)
                kept_f = lax.broadcasted_iota(jnp.int32, (events, ff_part), 0) < length
                slope[here, cols] = jnp.where(
                    kept_f, slope[here, cols].astype(F32) * d_hid[srow, cols], 0.0
                ).astype(BF16)
        dn = dot(proj[rows, :], wqkv[...])
        for m in range(mp):
            cols = slice(m * ff_part, (m + 1) * ff_part)
            dn = dn + dot(slope[rows, cols], wts[m, up0 : up0 + width, :], 1, 1)
        unit, inv = normalise(mixed[rows, :].astype(F32))
        center = jnp.mean(dn, axis=1, keepdims=True)
        along = jnp.mean(dn * unit, axis=1, keepdims=True)
        body = (dn - center - unit * along) * inv
        for s in range(per_block):
            i = b * per_block + s
            here = pl.ds(pl.multiple_of(b * block_rows + s * events, events), events)
            direct = jnp.where(row_w < lens[i], g_row[pl.ds(i, 1), :], 0.0)
            dmix[here, :] = (direct + body[s * events : (s + 1) * events]).astype(BF16)


def local(states, key_embed, partner, mix_numer, lengths, w_qkv, w_out, w_up, w_down, w_proj):
    sessions, ev_part, width = states.shape
    n = lax.axis_size("dp")
    mp = lax.axis_size("mp")
    cap = (sessions + n - 2) // (n - 1)
    slots = n * cap
    me = lax.axis_index("dp")
    total = partner.shape[0]
    chunk = sessions // mp
    events = ev_part * mp
    inner_part = w_qkv.shape[2]
    inner = inner_part * mp
    heads = inner // HD
    ff_part = w_up.shape[1]
    group = 8 if n % 8 == 0 else 2
    half = width // 2

    source = partner.reshape(n, sessions) // sessions
    ids = jnp.arange(sessions, dtype=jnp.int32)
    slot = jnp.sum(
        (
            (source[:, :, None] == source[:, None, :]) & (ids[None, None, :] < ids[None, :, None])
        ).astype(jnp.int32),
        axis=2,
    )
    code = (jnp.arange(n, dtype=jnp.int32)[:, None] * cap + slot).reshape(-1)
    rel = partner - me * sessions
    slot_ids = jnp.arange(slots, dtype=jnp.int32)
    mine = (rel >= 0) & (rel < sessions)
    send_code = jnp.sum(jnp.where(rel[None, :] == ids[:, None], code[None, :], 0), axis=1)
    send_idx = jnp.sum(
        jnp.where((code[None, :] == slot_ids[:, None]) & mine[None, :], rel[None, :], 0), axis=1
    )
    own_source = lax.dynamic_slice_in_dim(source, me, 1, 0)[0]
    recv_code = own_source * cap + lax.dynamic_slice_in_dim(slot, me, 1, 0)[0]
    recv_idx = jnp.sum(
        jnp.where(recv_code[None, :] == slot_ids[:, None], ids[None, :], 0), axis=1
    )
    smem = pl.BlockSpec(memory_space=pltpu.SMEM)
    vmem = pl.BlockSpec(memory_space=pltpu.VMEM)
    dma = pltpu.SemaphoreType.DMA

    mixed, all_keys, all_wts = pl.pallas_call(
        functools.partial(gather_kernel, n, mp, group, cap),
        out_shape=(
            jax.ShapeDtypeStruct((chunk, mp, ev_part, width), BF16),
            jax.ShapeDtypeStruct((total, key_embed.shape[1]), BF16),
            jax.ShapeDtypeStruct((mp, 4 * inner_part + width + ff_part, width), BF16),
        ),
        in_specs=[smem] * 3 + [vmem] * 6,
        out_specs=(vmem,) * 3,
        scratch_shapes=[
            pltpu.VMEM((2, slots, ev_part, half), BF16),
            pltpu.VMEM((slots, ev_part, half), BF16),
            pltpu.VMEM((slots, ev_part, half), BF16),
            pltpu.VMEM((2, sessions, ev_part, half), BF16),
            dma((2, n)), dma((2, n)), dma((n,)), dma((n,)),
            dma((2, mp)), dma((2, mp)), dma((mp,)), dma((mp,)),
            dma((mp, group)), dma((mp, group)), dma((mp,)), dma((mp,)),
        ],
        compiler_params=pltpu.CompilerParams(collective_id=0, has_side_effects=True),
    )(send_idx, recv_code, mix_numer, states, key_embed, w_qkv.transpose(0, 2, 1), w_out, w_up, w_down)

    rows = chunk * events
    per_block = min(8, chunk)
    dmix, loss = pl.pallas_call(
        functools.partial(layer_kernel, events, heads, per_block),
        out_shape=(
            jax.ShapeDtypeStruct((rows, width), BF16),
            jax.ShapeDtypeStruct((chunk, 128), F32),
        ),
        in_specs=[smem] * 3 + [vmem] * 4,
        out_specs=(vmem, vmem),
        scratch_shapes=[
            pltpu.VMEM((3 * inner, width), BF16),
            pltpu.VMEM((inner, width), BF16),
            pltpu.VMEM((rows, 3 * inner), BF16),
            pltpu.VMEM((rows, heads * events), F32),
            pltpu.VMEM((rows, mp * ff_part), BF16),
            pltpu.VMEM((chunk, mp * ff_part), F32),
            pltpu.VMEM((chunk, width), F32),
            pltpu.VMEM((chunk, inner), F32),
            pltpu.VMEM((chunk, mp * ff_part), F32),
            pltpu.VMEM((chunk, inner), F32),
            pltpu.VMEM((chunk, width), F32),
            pltpu.VMEM((4, chunk, 128), F32),
            pltpu.SMEM((chunk,), jnp.int32),
        ],
        compiler_params=pltpu.CompilerParams(vmem_limit_bytes=56 * 1024 * 1024),
    )(lengths, partner, mix_numer, mixed.reshape(rows, width), all_wts, all_keys, w_proj)

    dm_lo, dm_hi, arr_buf, all_loss = pl.pallas_call(
        functools.partial(return_kernel, n, mp, cap),
        out_shape=(
            jax.ShapeDtypeStruct((sessions, ev_part, half), BF16),
            jax.ShapeDtypeStruct((sessions, ev_part, half), BF16),
            jax.ShapeDtypeStruct((2, slots, ev_part, half), BF16),
            jax.ShapeDtypeStruct((sessions, 128), F32),
        ),
        in_specs=[smem] * 2 + [vmem] * 2,
        out_specs=(vmem,) * 4,
        scratch_shapes=[
            pltpu.VMEM((2, slots, ev_part, half), BF16),
            dma((2, mp)), dma((2, mp)), dma((mp,)), dma((mp,)), dma((2, n)), dma((2, n)),
        ],
        compiler_params=pltpu.CompilerParams(collective_id=1, has_side_effects=True),
    )(recv_idx, mix_numer, dmix.reshape(chunk, mp, ev_part, width), loss)

    block = chunk
    grad, loss_row = pl.pallas_call(
        final_kernel,
        grid=(sessions // block,),
        out_shape=(
            jax.ShapeDtypeStruct((sessions, ev_part, width), F32),
            jax.ShapeDtypeStruct((1, sessions), F32),
        ),
        in_specs=[
            smem,
            smem,
            pl.BlockSpec((block, ev_part, half), lambda b: (b, 0, 0)),
            pl.BlockSpec((block, ev_part, half), lambda b: (b, 0, 0)),
            pl.BlockSpec((2, slots, ev_part, half), lambda b: (0, 0, 0, 0)),
            pl.BlockSpec((sessions, 128), lambda b: (0, 0)),
        ],
        out_specs=(
            pl.BlockSpec((block, ev_part, width), lambda b: (b, 0, 0)),
            pl.BlockSpec((1, sessions), lambda b: (0, 0)),
        ),
    )(send_code, mix_numer, dm_lo, dm_hi, arr_buf, all_loss)
    return (loss_row.reshape(sessions), grad)


def solution(mesh):
    placed = (
        P("dp", "mp", None),
        P("dp", None),
        P(),
        P("dp"),
        P(),
        P(None, None, "mp"),
        P("mp", None),
        P(None, "mp"),
        P("mp", None),
        P(),
    )
    return jax.shard_map(
        local, mesh=mesh, in_specs=placed, out_specs=(P("dp"), P("dp", "mp", None)), check_vma=False
    )
```

```python
import functools

import jax
import jax.numpy as jnp
from jax import lax
from jax.experimental import pallas as pl
from jax.experimental.pallas import tpu as pltpu
from jax.sharding import PartitionSpec as P

HD = 64
SOFTMAX_TEMP = 0.1
LN_EPS = 1e-05
NORM_EPS = 1e-06
HIGHEST = lax.Precision.HIGHEST
MESH = pl.DeviceIdType.MESH
F32 = jnp.float32
BF16 = jnp.bfloat16


def remote(src, dst, send_sem, recv_sem, device):
    return pltpu.make_async_remote_copy(
        src_ref=src,
        dst_ref=dst,
        send_sem=send_sem,
        recv_sem=recv_sem,
        device_id=device,
        device_id_type=MESH,
    )


def greet(n, mp):
    me, mz = lax.axis_index("dp"), lax.axis_index("mp")
    barrier = pltpu.get_barrier_semaphore()
    for o in range(1, n):
        pl.semaphore_signal(
            barrier, inc=1, device_id={"dp": lax.rem(me + o, n)}, device_id_type=MESH
        )
    for o in range(1, mp):
        pl.semaphore_signal(
            barrier, inc=1, device_id={"mp": lax.rem(mz + o, mp)}, device_id_type=MESH
        )
    pl.semaphore_wait(barrier, n - 1 + mp - 1)


def gather_kernel(
    n, mp, group, cap,
    send_idx, recv_code, mix_num,
    states, keys, w_qkv, w_out, w_up, w_down,
    mixed, all_keys, all_wts,
    out_buf, in_lo, in_hi, mix_buf,
    dp_s, dp_r, key_s, key_r, mp_s, mp_r, wz_s, wz_r, wg_s, wg_r, wc_s, wc_r,
):
    me, mz = lax.axis_index("dp"), lax.axis_index("mp")
    in_buf = (in_lo, in_hi)
    sessions = states.shape[0]
    half = out_buf.shape[3]
    chunk = sessions // mp
    chips = group // 2
    piece = all_wts.shape[1] // group
    part_w = w_out.shape[0]
    width = states.shape[2]
    for j in range(3):
        all_wts[mz, j * part_w : (j + 1) * part_w, :] = w_qkv[j]
    all_wts[mz, 3 * part_w : 4 * part_w, :] = w_out[...]
    all_wts[mz, 4 * part_w : 4 * part_w + width, :] = w_up[...]
    all_wts[mz, 4 * part_w + width :, :] = w_down[...]
    place = lax.rem(me, group)
    base = me - place
    core = lax.rem(place, 2)
    chip = place // 2
    core_rows = pl.ds(pl.multiple_of(core * (chips * piece), piece), chips * piece)
    rows = pl.ds(pl.multiple_of((core * chips + chip) * piece, piece), piece)

    @pl.loop(0, n * cap, unroll=8)
    def _(j):
        i = send_idx[j]
        for h in range(2):
            out_buf[h, j] = states[i, :, h * half : (h + 1) * half]

    greet(n, mp)
    pending = []
    wz = []
    for o in range(1, mp):
        c = remote(
            all_wts.at[mz, rows], all_wts.at[mz, rows], wz_s.at[o], wz_r.at[o],
            {"mp": lax.rem(mz + o, mp)},
        )
        c.start()
        wz.append(c)
    dp = [[], []]
    for h in range(2):
        for o in range(1, n):
            peer = lax.rem(me + o, n)
            c = remote(
                out_buf.at[h, pl.ds(peer * cap, cap)], in_buf[h].at[pl.ds(me * cap, cap)],
                dp_s.at[h, o], dp_r.at[h, o], {"dp": peer},
            )
            c.start()
            dp[h].append(c)
    key_rows = pl.ds(pl.multiple_of(me * sessions, sessions), sessions)
    for o in range(1, n):
        c = remote(
            keys, all_keys.at[key_rows], key_s.at[o], key_r.at[o], {"dp": lax.rem(me + o, n)}
        )
        c.start()
        pending.append(c)
    all_keys[key_rows, :] = keys[...]
    plane = []
    for h in range(2):
        cols = slice(h * half, (h + 1) * half)
        for c in dp[h]:
            c.wait()

        @pl.loop(0, sessions, unroll=8)
        def _(i):
            w = mix_num[i].astype(F32) * 0.0625
            mix_buf[h, i] = (
                w * states[i, :, cols].astype(F32)
                + (1.0 - w) * in_buf[h][recv_code[i]].astype(F32)
            ).astype(BF16)

        for o in (2, 1, 3) if mp == 4 else range(1, mp):
            peer = lax.rem(mz + o, mp)
            c = remote(
                mix_buf.at[h, pl.ds(peer * chunk, chunk)],
                mixed.at[pl.ds(0, chunk), mz, :, cols],
                mp_s.at[h, o], mp_r.at[h, o], {"mp": peer},
            )
            c.start()
            pending.append(c)
        if h == 0:
            for o in range(1, mp):
                wz[o - 1].wait()
                held = lax.rem(mz + mp - o, mp)
                for g in range(1, chips):
                    peer = base + lax.rem(chip + g, chips) * 2 + core
                    c = remote(
                        all_wts.at[held, rows], all_wts.at[held, rows],
                        wg_s.at[o, g], wg_r.at[o, g], {"dp": peer},
                    )
                    c.start()
                    plane.append(c)

        @pl.loop(0, chunk, unroll=8)
        def _(i):
            mixed[i, mz, :, cols] = mix_buf[h, mz * chunk + i]

    for c in plane:
        c.wait()
    for o in range(1, mp):
        held = lax.rem(mz + mp - o, mp)
        c = remote(
            all_wts.at[held, core_rows], all_wts.at[held, core_rows],
            wc_s.at[o], wc_r.at[o], {"dp": me + 1 - 2 * core},
        )
        c.start()
        pending.append(c)
    for c in pending:
        c.wait()


def return_kernel(
    n, mp, cap,
    recv_idx, mix_num,
    dmix, loss,
    dm_lo, dm_hi, arr_buf, all_loss,
    ret_buf,
    mp_s, mp_r, ls_s, ls_r, dp_s, dp_r,
):
    me, mz = lax.axis_index("dp"), lax.axis_index("mp")
    chunk = dmix.shape[0]
    dm_buf = (dm_lo, dm_hi)
    half = dm_lo.shape[2]
    greet(n, mp)
    mine = pl.ds(pl.multiple_of(mz * chunk, chunk), chunk)
    first = [[], []]
    pending = []
    for h in range(2):
        for o in (2, 1, 3) if mp == 4 else range(1, mp):
            peer = lax.rem(mz + o, mp)
            c = remote(
                dmix.at[pl.ds(0, chunk), peer, :, h * half : (h + 1) * half],
                dm_buf[h].at[mine],
                mp_s.at[h, o], mp_r.at[h, o], {"mp": peer},
            )
            c.start()
            first[h].append(c)
    for o in range(1, mp):
        c = remote(
            loss, all_loss.at[mine], ls_s.at[o], ls_r.at[o], {"mp": lax.rem(mz + o, mp)}
        )
        c.start()
        pending.append(c)
    all_loss[mine, :] = loss[...]

    @pl.loop(0, chunk, unroll=8)
    def _(i):
        for h in range(2):
            dm_buf[h][mz * chunk + i] = dmix[i, mz, :, h * half : (h + 1) * half]

    for h in range(2):
        for c in first[h]:
            c.wait()

        @pl.loop(0, n * cap, unroll=8)
        def _(j):
            i = recv_idx[j]
            ret_buf[h, j] = (
                (1.0 - mix_num[i].astype(F32) * 0.0625) * dm_buf[h][i].astype(F32)
            ).astype(BF16)

        for o in range(1, n):
            peer = lax.rem(me + o, n)
            c = remote(
                ret_buf.at[h, pl.ds(peer * cap, cap)], arr_buf.at[h, pl.ds(me * cap, cap)],
                dp_s.at[h, o], dp_r.at[h, o], {"dp": peer},
            )
            c.start()
            pending.append(c)
    for c in pending:
        c.wait()


def final_kernel(send_code, mix_num, dm_lo, dm_hi, arr, all_loss, grad, loss):
    dm = (dm_lo, dm_hi)
    block, half = dm_lo.shape[0], dm_lo.shape[2]
    sessions = all_loss.shape[0]
    base = pl.program_id(0) * block
    for j in range(block):
        s = base + j
        weight = mix_num[s].astype(F32) * 0.0625
        for h in range(2):
            grad[j, :, h * half : (h + 1) * half] = (
                weight * dm[h][j].astype(F32) + arr[h, send_code[s]].astype(F32)
            )
    diagonal = lax.broadcasted_iota(
        jnp.int32, (sessions, sessions), 0
    ) == lax.broadcasted_iota(jnp.int32, (sessions, sessions), 1)
    loss[...] = jnp.sum(
        jnp.where(diagonal, all_loss[:, 0:sessions], 0.0), axis=0, keepdims=True
    )


def dot(a, b, ca=1, cb=0, precision=None):
    return lax.dot_general(
        a, b, (((ca,), (cb,)), ((), ())), precision=precision, preferred_element_type=F32
    )


def dot_split(a, b, cb=0):
    hi = a.astype(BF16)
    lo = (a - hi.astype(F32)).astype(BF16)
    return dot(hi, b, 1, cb) + dot(lo, b, 1, cb)


def layer_kernel(
    events, heads, per_block,
    lengths, partner, mix_num,
    mixed, wts, keys, w_proj,
    dmix, loss,
    wqkv, w_out, proj, probs, slope, hpool, xpool, ctx, d_hid, d_ctx, g_row, aux, lens,
):
    mp = wts.shape[0]
    width = mixed.shape[1]
    sessions = hpool.shape[0]
    first = lax.axis_index("mp") * sessions
    start = lax.axis_index("dp") * (mp * sessions) + first
    for i in range(sessions):
        other = partner[start + i]
        longest = jnp.maximum(lengths[start + i], lengths[other])
        lens[i] = longest
        row = slice(i, i + 1)
        shape = (1, aux.shape[2])
        aux[0, row, :] = jnp.full(shape, mix_num[first + i].astype(F32) * 0.0625, F32)
        aux[1, row, :] = jnp.full(shape, longest.astype(F32), F32)
        aux[2, row, :] = jnp.full(shape, (start + i).astype(F32), F32)
        aux[3, row, :] = jnp.full(shape, other.astype(F32), F32)
    inner = heads * HD
    part = inner // mp
    ff_part = wts.shape[1] - 4 * part - width
    up0 = 4 * part
    down0 = up0 + width
    lanes = heads * events
    block_rows = per_block * events
    for m in range(mp):
        for j in range(3):
            wqkv[j * inner + m * part : j * inner + (m + 1) * part, :] = wts[
                m, j * part : (j + 1) * part, :
            ]
        w_out[m * part : (m + 1) * part, :] = wts[m, 3 * part : 4 * part, :]
    head_mask = (
        lax.broadcasted_iota(jnp.int32, (lanes, inner), 0) // events
        == lax.broadcasted_iota(jnp.int32, (lanes, inner), 1) // HD
    )
    ones_blk = (
        lax.broadcasted_iota(jnp.int32, (lanes, lanes), 0) // events
        == lax.broadcasted_iota(jnp.int32, (lanes, lanes), 1) // events
    ).astype(F32).astype(BF16)
    row_t = lax.broadcasted_iota(jnp.int32, (events, lanes), 0)
    lane_r = lax.broadcasted_iota(jnp.int32, (events, lanes), 1) % events
    row_w = lax.broadcasted_iota(jnp.int32, (events, width), 0)
    pool_row = lax.broadcasted_iota(jnp.int32, (per_block, block_rows), 0)
    pool_lane = lax.broadcasted_iota(jnp.int32, (per_block, block_rows), 1)
    zero_b = jnp.zeros((lanes, inner), BF16)
    scale = HD ** (-0.5)
    c0 = 0.7978845608028654

    def spread(v):
        return jnp.where(head_mask, jnp.concatenate([v] * heads, axis=0), zero_b)

    def fold(full):
        kept = jnp.where(head_mask, full, 0.0)
        total = kept[0:events]
        for h in range(1, heads):
            total = total + kept[h * events : (h + 1) * events]
        return total

    def normalise(x):
        mean = jnp.mean(x, axis=1, keepdims=True)
        centered = x - mean
        inv = lax.rsqrt(jnp.mean(centered * centered, axis=1, keepdims=True) + LN_EPS)
        return centered * inv, inv

    @pl.loop(0, sessions // per_block)
    def _(b):
        rows = pl.ds(pl.multiple_of(b * block_rows, block_rows), block_rows)
        srows = pl.ds(pl.multiple_of(b * per_block, per_block), per_block)
        mixed_b = mixed[rows, :]
        unit, _inv = normalise(mixed_b.astype(F32))
        normed = unit.astype(BF16)
        qkv = dot(normed, wqkv[...], 1, 1).astype(BF16)
        proj[rows, :] = qkv
        len_col = aux[1, srows, 0:1]
        pool_mask = jnp.where(
            (pool_lane // events == pool_row)
            & ((pool_lane % events).astype(F32) < len_col),
            1.0,
            0.0,
        ).astype(BF16)
        xpool[srows, :] = dot(pool_mask, mixed_b) / len_col
        for m in range(mp):
            pre = dot(normed, wts[m, up0 : up0 + width, :])
            sq = pre * pre
            th = jnp.tanh(c0 * (pre + 0.044715 * (sq * pre)))
            half = 0.5 * (1.0 + th)
            act = (pre * half).astype(BF16)
            cols = slice(m * ff_part, (m + 1) * ff_part)
            slope[rows, cols] = (
                half + 0.5 * pre * (1.0 - th * th) * (c0 * (1.0 + 3 * 0.044715 * sq))
            ).astype(BF16)
            hpool[srows, cols] = dot(pool_mask, act) / len_col
        for s in range(per_block):
            length = lens[b * per_block + s]
            lo = s * events
            q = qkv[lo : lo + events, 0:inner]
            k = qkv[lo : lo + events, inner : 2 * inner]
            v = qkv[lo : lo + events, 2 * inner : 3 * inner]
            e = jnp.where(lane_r < length, jnp.exp(dot(q, spread(k), 1, 1) * scale), 0.0)
            p = e / dot_split(e, ones_blk)
            probs[pl.ds(pl.multiple_of(b * block_rows + lo, events), events), :] = p
            used = jnp.where(row_t < length, p.astype(BF16).astype(F32), 0.0)
            seen = jnp.sum(used, axis=0, keepdims=True)
            ctx[pl.ds(b * per_block + s, 1), :] = dot_split(
                jnp.broadcast_to(seen, (8, lanes)), spread(v)
            )[0:1] / length.astype(F32)

    weight, len_all = aux[0, :, 0:1], aux[1, :, 0:1]
    own_id, partner_id = aux[2, :, 0:1], aux[3, :, 0:1]
    pooled = xpool[...] + dot_split(ctx[...], w_out[...])
    for m in range(mp):
        cols = slice(m * ff_part, (m + 1) * ff_part)
        pooled = pooled + dot_split(hpool[:, cols], wts[m, down0 : down0 + ff_part, :])
    embed = dot_split(pooled, w_proj[...])
    inv_norm = lax.rsqrt(jnp.sum(embed * embed, axis=1, keepdims=True) + NORM_EPS)
    unit_q = embed * inv_norm
    keys_f = keys[...].astype(F32)
    unit_k = keys_f * lax.rsqrt(jnp.sum(keys_f * keys_f, axis=1, keepdims=True) + NORM_EPS)
    logits = dot(unit_q, unit_k, 1, 1, HIGHEST) / SOFTMAX_TEMP
    exp_l = jnp.exp(logits)
    sum_l = jnp.sum(exp_l, axis=1, keepdims=True)
    ids = lax.broadcasted_iota(jnp.int32, logits.shape, 1).astype(F32)
    wanted = jnp.where(ids == own_id, weight, 0.0) + jnp.where(
        ids == partner_id, 1.0 - weight, 0.0
    )
    loss[...] = jnp.broadcast_to(
        jnp.log(sum_l) - jnp.sum(wanted * logits, axis=1, keepdims=True), loss.shape
    )
    grad_u = dot(exp_l / sum_l - wanted, unit_k, 1, 0, HIGHEST) / SOFTMAX_TEMP
    grad_e = (grad_u - unit_q * jnp.sum(unit_q * grad_u, axis=1, keepdims=True)) * inv_norm
    g = dot_split(grad_e, w_proj[...], 1) * (1.0 / len_all)
    g_row[...] = g
    g_b = g.astype(BF16)
    for m in range(mp):
        d_hid[:, m * ff_part : (m + 1) * ff_part] = dot(
            g_b, wts[m, down0 : down0 + ff_part, :], 1, 1
        )
    d_ctx[...] = dot(g_b, w_out[...], 1, 1)

    @pl.loop(0, sessions // per_block)
    def _(b):
        rows = pl.ds(pl.multiple_of(b * block_rows, block_rows), block_rows)
        for s in range(per_block):
            i = b * per_block + s
            srow = pl.ds(i, 1)
            length = lens[i]
            here = pl.ds(pl.multiple_of(b * block_rows + s * events, events), events)
            q = proj[here, 0:inner]
            k = proj[here, inner : 2 * inner]
            v = proj[here, 2 * inner : 3 * inner]
            p = probs[here, :]
            dc = jnp.broadcast_to(d_ctx[srow, :].astype(BF16), (events, inner))
            u = dot(dc, spread(v), 1, 1)
            kept = row_t < length
            d_score = jnp.where(
                kept, p * (u - dot_split(p * u, ones_blk)) * scale, 0.0
            ).astype(BF16)
            used = jnp.where(kept, p, 0.0).astype(BF16)
            proj[here, 0:inner] = dot(d_score, spread(k)).astype(BF16)
            proj[here, inner : 2 * inner] = fold(dot(d_score, q, 0, 0)).astype(BF16)
            proj[here, 2 * inner : 3 * inner] = fold(dot(used, dc, 0, 0)).astype(BF16)
            for m in range(mp):
                cols = slice(m * ff_part, (m + 1) * ff_part)
                kept_f = lax.broadcasted_iota(jnp.int32, (events, ff_part), 0) < length
                slope[here, cols] = jnp.where(
                    kept_f, slope[here, cols].astype(F32) * d_hid[srow, cols], 0.0
                ).astype(BF16)
        dn = dot(proj[rows, :], wqkv[...])
        for m in range(mp):
            cols = slice(m * ff_part, (m + 1) * ff_part)
            dn = dn + dot(slope[rows, cols], wts[m, up0 : up0 + width, :], 1, 1)
        unit, inv = normalise(mixed[rows, :].astype(F32))
        center = jnp.mean(dn, axis=1, keepdims=True)
        along = jnp.mean(dn * unit, axis=1, keepdims=True)
        body = (dn - center - unit * along) * inv
        for s in range(per_block):
            i = b * per_block + s
            here = pl.ds(pl.multiple_of(b * block_rows + s * events, events), events)
            direct = jnp.where(row_w < lens[i], g_row[pl.ds(i, 1), :], 0.0)
            dmix[here, :] = (direct + body[s * events : (s + 1) * events]).astype(BF16)


def local(states, key_embed, partner, mix_numer, lengths, w_qkv, w_out, w_up, w_down, w_proj):
    sessions, ev_part, width = states.shape
    n = lax.axis_size("dp")
    mp = lax.axis_size("mp")
    cap = (sessions + n - 2) // (n - 1)
    slots = n * cap
    me = lax.axis_index("dp")
    total = partner.shape[0]
    chunk = sessions // mp
    events = ev_part * mp
    inner_part = w_qkv.shape[2]
    inner = inner_part * mp
    heads = inner // HD
    ff_part = w_up.shape[1]
    group = 8 if n % 8 == 0 else 2
    half = width // 2

    source = partner.reshape(n, sessions) // sessions
    ids = jnp.arange(sessions, dtype=jnp.int32)
    slot = jnp.sum(
        (
            (source[:, :, None] == source[:, None, :]) & (ids[None, None, :] < ids[None, :, None])
        ).astype(jnp.int32),
        axis=2,
    )
    code = (jnp.arange(n, dtype=jnp.int32)[:, None] * cap + slot).reshape(-1)
    rel = partner - me * sessions
    slot_ids = jnp.arange(slots, dtype=jnp.int32)
    mine = (rel >= 0) & (rel < sessions)
    send_code = jnp.sum(jnp.where(rel[None, :] == ids[:, None], code[None, :], 0), axis=1)
    send_idx = jnp.sum(
        jnp.where((code[None, :] == slot_ids[:, None]) & mine[None, :], rel[None, :], 0), axis=1
    )
    own_source = lax.dynamic_slice_in_dim(source, me, 1, 0)[0]
    recv_code = own_source * cap + lax.dynamic_slice_in_dim(slot, me, 1, 0)[0]
    recv_idx = jnp.sum(
        jnp.where(recv_code[None, :] == slot_ids[:, None], ids[None, :], 0), axis=1
    )
    smem = pl.BlockSpec(memory_space=pltpu.SMEM)
    vmem = pl.BlockSpec(memory_space=pltpu.VMEM)
    dma = pltpu.SemaphoreType.DMA

    mixed, all_keys, all_wts = pl.pallas_call(
        functools.partial(gather_kernel, n, mp, group, cap),
        out_shape=(
            jax.ShapeDtypeStruct((chunk, mp, ev_part, width), BF16),
            jax.ShapeDtypeStruct((total, key_embed.shape[1]), BF16),
            jax.ShapeDtypeStruct((mp, 4 * inner_part + width + ff_part, width), BF16),
        ),
        in_specs=[smem] * 3 + [vmem] * 6,
        out_specs=(vmem,) * 3,
        scratch_shapes=[
            pltpu.VMEM((2, slots, ev_part, half), BF16),
            pltpu.VMEM((slots, ev_part, half), BF16),
            pltpu.VMEM((slots, ev_part, half), BF16),
            pltpu.VMEM((2, sessions, ev_part, half), BF16),
            dma((2, n)), dma((2, n)), dma((n,)), dma((n,)),
            dma((2, mp)), dma((2, mp)), dma((mp,)), dma((mp,)),
            dma((mp, group)), dma((mp, group)), dma((mp,)), dma((mp,)),
        ],
        compiler_params=pltpu.CompilerParams(collective_id=0, has_side_effects=True),
    )(send_idx, recv_code, mix_numer, states, key_embed, w_qkv.transpose(0, 2, 1), w_out, w_up, w_down)

    rows = chunk * events
    per_block = min(8, chunk)
    dmix, loss = pl.pallas_call(
        functools.partial(layer_kernel, events, heads, per_block),
        out_shape=(
            jax.ShapeDtypeStruct((rows, width), BF16),
            jax.ShapeDtypeStruct((chunk, 128), F32),
        ),
        in_specs=[smem] * 3 + [vmem] * 4,
        out_specs=(vmem, vmem),
        scratch_shapes=[
            pltpu.VMEM((3 * inner, width), BF16),
            pltpu.VMEM((inner, width), BF16),
            pltpu.VMEM((rows, 3 * inner), BF16),
            pltpu.VMEM((rows, heads * events), F32),
            pltpu.VMEM((rows, mp * ff_part), BF16),
            pltpu.VMEM((chunk, mp * ff_part), F32),
            pltpu.VMEM((chunk, width), F32),
            pltpu.VMEM((chunk, inner), F32),
            pltpu.VMEM((chunk, mp * ff_part), F32),
            pltpu.VMEM((chunk, inner), F32),
            pltpu.VMEM((chunk, width), F32),
            pltpu.VMEM((4, chunk, 128), F32),
            pltpu.SMEM((chunk,), jnp.int32),
        ],
        compiler_params=pltpu.CompilerParams(vmem_limit_bytes=56 * 1024 * 1024),
    )(lengths, partner, mix_numer, mixed.reshape(rows, width), all_wts, all_keys, w_proj)

    dm_lo, dm_hi, arr_buf, all_loss = pl.pallas_call(
        functools.partial(return_kernel, n, mp, cap),
        out_shape=(
            jax.ShapeDtypeStruct((sessions, ev_part, half), BF16),
            jax.ShapeDtypeStruct((sessions, ev_part, half), BF16),
            jax.ShapeDtypeStruct((2, slots, ev_part, half), BF16),
            jax.ShapeDtypeStruct((sessions, 128), F32),
        ),
        in_specs=[smem] * 2 + [vmem] * 2,
        out_specs=(vmem,) * 4,
        scratch_shapes=[
            pltpu.VMEM((2, slots, ev_part, half), BF16),
            dma((2, mp)), dma((2, mp)), dma((mp,)), dma((mp,)), dma((2, n)), dma((2, n)),
        ],
        compiler_params=pltpu.CompilerParams(collective_id=1, has_side_effects=True),
    )(recv_idx, mix_numer, dmix.reshape(chunk, mp, ev_part, width), loss)

    block = chunk
    grad, loss_row = pl.pallas_call(
        final_kernel,
        grid=(sessions // block,),
        out_shape=(
            jax.ShapeDtypeStruct((sessions, ev_part, width), F32),
            jax.ShapeDtypeStruct((1, sessions), F32),
        ),
        in_specs=[
            smem,
            smem,
            pl.BlockSpec((block, ev_part, half), lambda b: (b, 0, 0)),
            pl.BlockSpec((block, ev_part, half), lambda b: (b, 0, 0)),
            pl.BlockSpec((2, slots, ev_part, half), lambda b: (0, 0, 0, 0)),
            pl.BlockSpec((sessions, 128), lambda b: (0, 0)),
        ],
        out_specs=(
            pl.BlockSpec((block, ev_part, width), lambda b: (b, 0, 0)),
            pl.BlockSpec((1, sessions), lambda b: (0, 0)),
        ),
    )(send_code, mix_numer, dm_lo, dm_hi, arr_buf, all_loss)
    return (loss_row.reshape(sessions), grad)


def solution(mesh):
    placed = (
        P("dp", "mp", None),
        P("dp", None),
        P(),
        P("dp"),
        P(),
        P(None, None, "mp"),
        P("mp", None),
        P(None, "mp"),
        P("mp", None),
        P(),
    )
    return jax.shard_map(
        local, mesh=mesh, in_specs=placed, out_specs=(P("dp"), P("dp", "mp", None)), check_vma=False
    )
```
